256 devices in a mesh: context: 4 (over y), expert: 64 (over x, z, core).
Axes of the slice: x: 4, y: 4, z: 8, core: 2. Of those that a mesh axis runs over, the one named last changes fastest.
Arguments:
- queries: bfloat16 [512, 24576], P(None, 'expert'), may hold values from -14 to 14
- key_lift: bfloat16 [128, 128, 512], P('expert'), may hold values from -0.5 to 0.5
- value_lift: bfloat16 [128, 512, 128], P('expert'), may hold values from -0.25 to 0.25
- page_pool: bfloat16 [16, 64, 576], P('context'), may hold values from -6 to 6
- fresh_latents: bfloat16 [64, 8, 576], P('context'), may hold values from -6 to 6
- page_table: int32 [64, 12], replicated, may hold values from 0 to 15, as said below
- context_lengths: int32 [64], replicated, may hold values from 705 to 768, as said below
- tree_parents: int32 [64, 8], replicated, may hold values from -1 to 6, as said below
- out_weight: bfloat16 [16384, 7168], P('expert', 'context'), may hold values from -0.5 to 0.5
- residual: bfloat16 [512, 7168], P('expert', 'context'), may hold values from -6 to 6
- norm_gain: float32 [7168], replicated, may hold values from 0.5 to 2
- expert_ids: int32 [512, 8], P('expert'), may hold values from 0 to 63, all different within a row; in each aligned block of 8 rows (0 to 7, 8 to 15, ...) at most 3 rows name the same one
- route_weights: float32 [512, 8], P('expert'), may hold values from 0.1 to 0.6
- gate_matrix: bfloat16 [64, 7168, 1024], P('expert', None, 'context'), may hold values from -0.0625 to 0.0625
- up_matrix: bfloat16 [64, 7168, 1024], P('expert', None, 'context'), may hold values from -0.0625 to 0.0625
- down_matrix: bfloat16 [64, 1024, 7168], P('expert', 'context'), may hold values from -0.1875 to 0.1875
Outputs:
- layer_out: bfloat16 [512, 7168], P('expert', 'context')
The draws below stay inside these ranges and needn't reach their ends.
Inputs may be any that keep to these rules, and one draw needn't show every extreme that they name: `page_table`: the 12 pages of a leaf are distinct. `context_lengths`: entry k of a leaf's page table holds its context tokens k * 64 to k * 64 + 63; some leaf fills all 12 pages. `tree_parents`: token 0 of a leaf has parent -1; token t > 0 has a parent among tokens 0 to t - 1 of the same leaf. `expert_ids`: within each aligned block of 8 rows, no expert is named by more than 3 rows, a bound that some block reaches.
All inputs are finite; a program needn't handle non-finite values.
Results may differ from the reference program's by a relative error of at most 0.011.
Values may be sent and summed in bfloat16 or wider, within the bound.
No kernel may reach another device: no remote copies, remote signals or barrier semaphores. Data moves between devices by JAX's collectives and lax.ppermute only.
A program may use at most 64 MiB of HBM per device.

```python
import math
import jax
import jax.numpy as jnp
import numpy as np
from jax import lax

D = 7168
LAT = 512
ROPE = 64
QK = 128
VD = 128
FFE = 1024
TOPK = 8
LOOK = 8
PAGE = 64
MAXP = 12
ROW_DEV = 8
HEADS = 128
EXPERTS = 64
CKV = 576
ROWS = 512
LEAVES = 64
POOL = 16
CAP = 3


def draw_queries(key, part):
    full_shape = (ROWS, HEADS, QK + ROPE)
    sample = jnp.clip(jax.random.normal(jax.random.fold_in(key, 12), full_shape, jnp.float32), -6.0, 6.0)
    return sample.reshape(ROWS, HEADS * (QK + ROPE)).astype(jnp.bfloat16)


def draw_page_pool(key, part):
    full_shape = (POOL, PAGE, LAT + ROPE)
    sample = jnp.clip(jax.random.normal(jax.random.fold_in(key, 14), full_shape, jnp.float32), -6.0, 6.0)
    return sample.astype(jnp.bfloat16)


def draw_page_table(key, part):
    leaf_keys = jax.random.split(jax.random.fold_in(key, 21), LEAVES)

    def shuffle(leaf_key):
        return jax.random.permutation(leaf_key, POOL)
    orders = jax.vmap(shuffle)(leaf_keys)
    return orders[:, :MAXP].astype(jnp.int32)


def draw_context_lengths(key, part):
    drawn_len = jax.random.randint(jax.random.fold_in(key, 22), (LEAVES,), (MAXP - 1) * PAGE + 1, MAXP * PAGE + 1)
    return jnp.where(jnp.arange(LEAVES) == 0, MAXP * PAGE, drawn_len).astype(jnp.int32)


def draw_tree_parents(key, part):
    positions = jnp.arange(LOOK)
    upper_bound = jnp.maximum(positions, 1)
    parents_drawn = jax.random.randint(jax.random.fold_in(key, 23), (LEAVES, LOOK), 0, upper_bound[None, :])
    return jnp.where(positions[None, :] == 0, -1, parents_drawn).astype(jnp.int32)


def block_levels(own_key, shape, cuts, smallest, largest):
    level = 1.0
    for axis_at, shards_of in cuts:
        steps = jax.random.uniform(jax.random.fold_in(jax.random.fold_in(own_key, 6), axis_at), (shards_of,), jnp.float32, smallest / len(cuts), largest / len(cuts))
        level = level * jnp.repeat(jnp.exp(steps), shape[axis_at] // shards_of).reshape((-1,) + (1,) * (len(shape) - 1 - axis_at))
    return level


def routed_block(own_key, own, number, rows, number_of, top, most, slope):
    sequence = jax.random.permutation(own_key, number_of)
    packed, common = shares(number_of, rows * top, most, slope, True), shares(number_of, rows * top, most, slope, False)
    places = jnp.arange(number_of)

    def named(tallies, offset_by):
        used = int((tallies > 0).sum())
        fixed = max(1, used // 4)
        passed = fixed + (places - fixed + offset_by * (used - fixed)) % max(1, number_of - fixed)
        return jnp.zeros((number_of,), jnp.int32).at[sequence[jnp.where(places < fixed, places, passed)]].set(jnp.asarray(tallies, jnp.int32))

    tallies = jnp.where(number % 4 == 0, named(packed, number // 4), named(common, number - number // 4 - 1))
    mixed = jax.random.permutation(jax.random.fold_in(own, 3), number_of)
    source_of, taker = mixed[0:number_of // 2 * 2:2], mixed[1:number_of // 2 * 2:2]
    slack = jnp.minimum(tallies[source_of] - 1, most - tallies[taker]) // 2
    slack = jnp.where((source_of == sequence[0]) | (taker == sequence[0]) | (tallies[taker] == 0), 0, jnp.maximum(slack, 0))
    passed = jax.random.randint(jax.random.fold_in(own, 4), (number_of // 2,), 0, 1 << 20) % (slack + 1)
    tallies = tallies.at[source_of].add(-passed).at[taker].add(passed)
    items = jnp.searchsorted(jnp.cumsum(tallies), jnp.arange(rows * top), side="right").astype(jnp.int32)
    table = items.reshape(top, rows).T
    table = table[jax.random.permutation(jax.random.fold_in(own, 1), rows)]
    offset_by = jax.random.randint(jax.random.fold_in(own, 2), (rows, 1), 0, top)
    return jnp.take_along_axis(table, (jnp.arange(top)[None, :] + offset_by) % top, axis=1)


def shares(number_of, total, bound, lean, full):
    weights = [(1 << 20) // math.isqrt(rank ** lean) + 1 for rank in range(1, number_of + 1)]
    largest = bound if full else min(bound, max(-(-total // number_of), total * weights[0] // sum(weights)))
    least = 1 if total - largest >= number_of - 1 else 0
    holding, spare = [largest] + [least] * (number_of - 1), total - largest - least * (number_of - 1)
    while spare > 0:
        candidates = [i for i in range(1, number_of) if holding[i] < largest] or [i for i in range(1, number_of) if holding[i] < bound]
        whole, budget = sum([weights[i] for i in candidates]), spare
        for i in candidates:
            extra = min(bound - holding[i], max(1, budget * weights[i] // whole), spare)
            holding[i] = holding[i] + extra
            spare = spare - extra
    return np.array(holding)


def noise(rng, dims, deviation, reach, cuts=(), held_as=jnp.bfloat16):
    gain = block_levels(rng, dims, cuts, -0.22, 0.18) if cuts else 1.0
    result = jax.random.normal(rng, dims, jnp.float32) * deviation * gain
    return jnp.minimum(jnp.maximum(result, -reach), reach).astype(held_as)


def setup_inputs(seed: int = 0) -> dict:
    keys = jax.random.split(jax.random.key(seed), 17)
    queries = draw_queries(jax.random.fold_in(keys[16], 71), 0)
    key_lift = noise(keys[1], (HEADS, QK, LAT), QK ** -0.5, 0.5, ((0, 64),))
    value_lift = noise(keys[2], (HEADS, LAT, VD), LAT ** -0.5, 0.25, ((0, 64),))
    page_pool = draw_page_pool(jax.random.fold_in(keys[16], 71), 0)
    fresh_latents = noise(keys[4], (LEAVES, LOOK, CKV), 1.5, 6.0, ((0, 4),))
    page_table = draw_page_table(jax.random.fold_in(keys[16], 71), 0)
    context_lengths = draw_context_lengths(jax.random.fold_in(keys[16], 71), 0)
    tree_parents = draw_tree_parents(jax.random.fold_in(keys[16], 71), 0)
    out_weight = noise(keys[8], (HEADS * VD, D), VD ** -0.5, 0.5, ((0, 64), (1, 4)))
    residual = noise(keys[9], (ROWS, D), 1.0, 6.0, ((0, 64), (1, 4)))
    norm_gain = jnp.clip(jnp.exp(jax.random.uniform(keys[10], (D,), jnp.float32, math.log(0.5), math.log(2.0))), 0.5, 2.0)
    expert_ids_keys = jax.random.split(jax.random.fold_in(keys[11], 1), ROWS // ROW_DEV)
    expert_ids_turns = jax.random.permutation(jax.random.fold_in(keys[11], 3), ROWS // ROW_DEV)
    expert_ids = jax.vmap(lambda own, number: routed_block(jax.random.fold_in(keys[11], 2), own, number, ROW_DEV, EXPERTS, TOPK, CAP, 2))(expert_ids_keys, expert_ids_turns).reshape((ROWS, TOPK))
    route_weights = jnp.clip(0.1 + 0.5 * jax.random.uniform(keys[12], (ROWS, TOPK), jnp.float32) ** block_levels(keys[12], (ROWS, TOPK), ((0, 64),), -0.2, 0.2), 0.1, 0.6)
    gate_matrix = noise(keys[13], (EXPERTS, D, FFE), D ** -0.5, 0.0625, ((0, 64), (2, 4)))
    up_matrix = noise(keys[14], (EXPERTS, D, FFE), D ** -0.5, 0.0625, ((0, 64), (2, 4)))
    down_matrix = noise(keys[15], (EXPERTS, FFE, D), FFE ** -0.5, 0.1875, ((0, 64), (1, 4)))
    return dict(queries=queries, key_lift=key_lift, value_lift=value_lift, page_pool=page_pool, fresh_latents=fresh_latents, page_table=page_table, context_lengths=context_lengths, tree_parents=tree_parents, out_weight=out_weight, residual=residual, norm_gain=norm_gain, expert_ids=expert_ids, route_weights=route_weights, gate_matrix=gate_matrix, up_matrix=up_matrix, down_matrix=down_matrix)


NEGATIVE_FILL = -1e+30
NORM_EPSILON = 1e-06

def ancestry(tree_parents):
    advance = tree_parents.shape[1]
    positions = jnp.arange(advance, dtype=jnp.int32)
    current = jnp.broadcast_to(positions[None, :], tree_parents.shape).astype(jnp.int32)
    linked = current[:, :, None] == positions[None, None, :]
    for repeat in range(advance - 1):
        climbed = jnp.take_along_axis(tree_parents, jnp.maximum(current, 0), axis=1)
        current = jnp.where(current >= 0, climbed, -1).astype(jnp.int32)
        linked = linked | (current[:, :, None] == positions[None, None, :])
    return linked

def page_limits(page_table, context_lengths, first_page, page_count, page_len):
    page_ids = first_page + jnp.arange(page_count, dtype=jnp.int32)
    matches = page_table[:, :, None] == page_ids[None, None, :]
    offsets = jnp.arange(page_table.shape[1], dtype=jnp.int32) * page_len
    remain = context_lengths[:, None] - offsets[None, :]
    return lax.optimization_barrier(jnp.sum(jnp.where(matches, remain[:, :, None], 0), axis=1)).astype(jnp.int32)

def context_mask(limits, page_len, advance):
    within = jnp.arange(page_len, dtype=jnp.int32)
    visible = within[None, None, :] < limits[:, :, None]
    visible = visible.reshape(limits.shape[0], -1)
    return jnp.repeat(visible, advance, axis=0)

def normalize(values, norm_gain):
    floats = values.astype(jnp.float32)
    inverse = lax.rsqrt(lax.optimization_barrier(jnp.mean(floats * floats, axis=-1, keepdims=True)) + NORM_EPSILON)
    return (floats * inverse * norm_gain).astype(jnp.bfloat16)

def reference(queries, key_lift, value_lift, page_pool, fresh_latents, page_table, context_lengths, tree_parents, out_weight, residual, norm_gain, expert_ids, route_weights, gate_matrix, up_matrix, down_matrix):
    score_scale = (QK + ROPE) ** (-0.5)
    shaped = queries.reshape(ROWS, HEADS, QK + ROPE)
    limits = page_limits(page_table, context_lengths, 0, POOL, PAGE)
    row_mask = context_mask(limits, PAGE, LOOK)
    fresh_mask = ancestry(tree_parents)
    flat_keys = page_pool.reshape(POOL * PAGE, LAT + ROPE)
    fresh_float = fresh_latents.astype(jnp.float32)

    def one_head(head_items):
        head_query, lift_keys, lift_values = head_items
        latent = jnp.dot(head_query[:, :QK], lift_keys, preferred_element_type=jnp.float32).astype(jnp.bfloat16)
        joined_query = jnp.concatenate([latent, head_query[:, QK:]], axis=1)
        page_scores = jnp.dot(joined_query, flat_keys.T, preferred_element_type=jnp.float32) * score_scale
        page_scores = jnp.where(row_mask, page_scores, NEGATIVE_FILL)
        grouped = joined_query.reshape(LEAVES, LOOK, LAT + ROPE).astype(jnp.float32)
        fresh_scores = jnp.einsum('ltc,lsc->lts', grouped, fresh_float, precision=lax.Precision.HIGHEST) * score_scale
        fresh_scores = jnp.where(fresh_mask, fresh_scores, NEGATIVE_FILL)
        row_max = jnp.maximum(lax.optimization_barrier(jnp.max(page_scores, axis=1)), lax.optimization_barrier(jnp.max(fresh_scores, axis=2)).reshape(ROWS))
        page_exp = jnp.exp(page_scores - row_max[:, None])
        fresh_exp = jnp.exp(fresh_scores - row_max.reshape(LEAVES, LOOK)[:, :, None])
        totals = lax.optimization_barrier(jnp.sum(page_exp, axis=1)) + lax.optimization_barrier(jnp.sum(fresh_exp, axis=2)).reshape(ROWS)
        numerators = jnp.dot(page_exp.astype(jnp.bfloat16), flat_keys[:, :LAT], preferred_element_type=jnp.float32)
        fresh_numer = jnp.einsum('lts,lsc->ltc', fresh_exp.astype(jnp.bfloat16).astype(jnp.float32), fresh_float[:, :, :LAT], precision=lax.Precision.HIGHEST)
        numerators = numerators + fresh_numer.reshape(ROWS, LAT)
        projected = jnp.dot(numerators, lift_values.astype(jnp.float32), precision=lax.Precision.HIGHEST)
        return (projected / totals[:, None]).astype(jnp.bfloat16)
    attention = lax.map(one_head, (jnp.transpose(shaped, (1, 0, 2)), key_lift, value_lift))
    attention = jnp.transpose(attention, (1, 0, 2)).reshape(ROWS, HEADS * VD)
    head_output = jnp.dot(attention, out_weight, preferred_element_type=jnp.float32)
    hidden_state = (residual.astype(jnp.float32) + head_output).astype(jnp.bfloat16)
    normed = normalize(hidden_state, norm_gain)
    blocks = ROWS // ROW_DEV
    grouped_ids = expert_ids.reshape(blocks, ROW_DEV * TOPK)
    onehot = (grouped_ids[:, :, None] == jnp.arange(EXPERTS, dtype=jnp.int32)[None, None, :]).astype(jnp.int32)
    earlier = jnp.cumsum(onehot, axis=1) - onehot
    slot_index = lax.optimization_barrier(jnp.sum(earlier * onehot, axis=2)).astype(jnp.int32)
    column = (jnp.arange(blocks, dtype=jnp.int32)[:, None] * CAP + slot_index).reshape(-1).astype(jnp.int32)
    owners = (jnp.arange(ROWS * TOPK, dtype=jnp.int32) // TOPK).astype(jnp.int32)
    flat_ids = expert_ids.reshape(-1).astype(jnp.int32)
    slot_table = jnp.full((EXPERTS, blocks * CAP), ROWS, dtype=jnp.int32).at[flat_ids, column].set(owners)
    padded = jnp.concatenate([normed, jnp.zeros((1, D), jnp.bfloat16)], axis=0)

    def one_expert(expert_items):
        rows_index, gate_cols, up_cols, down_rows = expert_items
        inputs = padded[rows_index]
        gate_part = jnp.dot(inputs, gate_cols, preferred_element_type=jnp.float32)
        up_part = jnp.dot(inputs, up_cols, preferred_element_type=jnp.float32)
        active = (jax.nn.silu(gate_part) * up_part).astype(jnp.bfloat16)
        return jnp.dot(active, down_rows, preferred_element_type=jnp.float32).astype(jnp.bfloat16)
    results = lax.map(one_expert, (slot_table, gate_matrix, up_matrix, down_matrix))
    picked = results[flat_ids, column].reshape(ROWS, TOPK, D).astype(jnp.float32)
    mixed_sum = lax.optimization_barrier(jnp.sum(route_weights[:, :, None] * picked, axis=1))
    return (hidden_state.astype(jnp.float32) + mixed_sum).astype(jnp.bfloat16)
```

```python
import jax
import jax.numpy as jnp
from jax import lax
from jax.experimental import pallas as pl
from jax.experimental.pallas import tpu as pltpu
from jax.sharding import Mesh, PartitionSpec as P

LAT = 512
ROPE = 64
QK = 128
VD = 128
PAGE = 64
LOOK = 8
CAP = 3
NEGATIVE_FILL = -1e30
NORM_EPSILON = 1e-06
F32 = jnp.float32
BF16 = jnp.bfloat16
SMEM = pl.BlockSpec(memory_space=pltpu.SMEM)
VMEM = pl.BlockSpec(memory_space=pltpu.VMEM)
TAIL = 128

CONTEXT = "context"
ROW_AXES = ("x", "z")
CORE = "core"
EXPERT = ("x", "z", "core")


def iota(shape, axis):
    return lax.broadcasted_iota(jnp.int32, shape, axis)


def dot_nn(a, b):
    return jnp.dot(a, b, preferred_element_type=F32)


def dot_nt(a, b):
    return lax.dot_general(a, b, (((1,), (1,)), ((), ())), preferred_element_type=F32)


def dot_tn(a, b):
    return lax.dot_general(a, b, (((0,), (0,)), ((), ())), preferred_element_type=F32)


def split3(value):
    high = value.astype(BF16)
    rest = value - high.astype(F32)
    middle = rest.astype(BF16)
    low = (rest - middle.astype(F32)).astype(BF16)
    return high, middle, low


def attention_kernel(
    place, q_ref, kl_ref, vl_ref, pool_ref, fresh_ref, table_ref, length_ref, parent_ref, *outs
):
    context = place[0]
    pool_rows = pool_ref.shape[0]
    fresh_rows = fresh_ref.shape[0]
    rows = q_ref.shape[0]
    leaves, table_len = table_ref.shape
    pages = pool_rows // PAGE
    lengths = jnp.sum(
        jnp.where(
            iota((leaves, leaves), 0) == iota((leaves, leaves), 1),
            length_ref[...].astype(F32),
            0.0,
        ),
        axis=1,
        keepdims=True,
    )
    remain = lengths - (iota((leaves, table_len), 1) * PAGE).astype(F32)
    remain = jnp.clip(remain, 0.0, float(PAGE))
    table = table_ref[...]
    lane = iota((leaves, 128), 1)
    limits = jnp.zeros((leaves, 128), F32)
    for page in range(pages):
        seen = jnp.sum(
            jnp.where(table == context * pages + page, remain, 0.0), axis=1, keepdims=True
        )
        limits = jnp.where(lane == page, seen, limits)
    spread = (iota((leaves, rows), 0) == iota((leaves, rows), 1) // LOOK).astype(F32).astype(BF16)
    row_limits = dot_nn(limits.T.astype(BF16), spread)
    page_limit = jnp.concatenate(
        [jnp.broadcast_to(row_limits[p : p + 1, :], (PAGE, rows)) for p in range(pages)], axis=0
    )
    within = jnp.bitwise_and(iota((pool_rows, rows), 0), PAGE - 1).astype(F32)
    page_mask = jnp.where(within < page_limit, 1.0, 0.0)
    own_leaves = fresh_rows // LOOK
    pick_leaf = (
        (iota((fresh_rows, leaves), 1) == context * own_leaves + iota((fresh_rows, leaves), 0) // LOOK)
        .astype(F32)
        .astype(BF16)
    )
    parents = dot_nn(pick_leaf, parent_ref[...].astype(F32).astype(BF16))
    token = jnp.bitwise_and(iota((fresh_rows, LOOK), 0), LOOK - 1)
    parent = jnp.sum(
        jnp.where(iota((fresh_rows, LOOK), 1) == token, parents, 0.0), axis=1, keepdims=True
    )
    square = (fresh_rows, fresh_rows)
    first = (iota(square, 0) // LOOK) * LOOK
    step = (iota(square, 1) - first).astype(F32)
    linked = jnp.where((step == parent) & (parent >= 0.0), 1.0, 0.0)
    linked = jnp.where(iota(square, 0) == iota(square, 1), 1.0, linked)
    for repeat in range(3):
        half = linked.astype(BF16)
        linked = jnp.where(dot_nn(half, half) > 0.5, 1.0, 0.0)
    fresh_mask = jnp.concatenate([linked.T] * (rows // fresh_rows), axis=1)
    here = iota((fresh_rows, rows), 1) // fresh_rows == context
    fresh_mask = jnp.where(here, fresh_mask, 0.0)
    mask = jnp.concatenate([page_mask, fresh_mask], axis=0) > 0.5

    keys = jnp.concatenate([pool_ref[...], fresh_ref[...]], axis=0)
    latents = keys[:, :LAT]
    turned = keys[:, LAT:]
    scale = (QK + ROPE) ** (-0.5)
    for head, out in enumerate(outs):
        start = head * (QK + ROPE)
        plain = q_ref[:, start : start + QK]
        rotary = q_ref[:, start + QK : start + QK + ROPE]
        lifted = dot_nn(plain, kl_ref[head]).astype(BF16)
        scores = (dot_nt(latents, lifted) + dot_nt(turned, rotary)) * scale
        scores = jnp.where(mask, scores, NEGATIVE_FILL)
        best = jnp.max(scores, axis=0, keepdims=True)
        weights = jnp.exp(scores - best)
        total = jnp.sum(weights, axis=0, keepdims=True)
        values = dot_nn(latents, vl_ref[head]).T.astype(BF16)
        mixed = dot_nn(values, weights.astype(BF16)) / total
        out[:VD, :] = mixed.astype(BF16)
        high, middle, low = split3(best + jnp.log(total))
        line = iota((16, rows), 0)
        extra = jnp.where(
            line == 0,
            high.astype(F32),
            jnp.where(line == 1, middle.astype(F32), jnp.where(line == 2, low.astype(F32), 0.0)),
        )
        out[VD:, :] = extra.astype(BF16)


def merge_kernel(place, *refs):
    core = place[2]
    parts, (weight_ref, send_ref, keep_ref, scratch) = refs[:8], refs[8:]
    heads = []
    for head in range(2):
        own = parts[4 * head : 4 * head + 4]
        logs = []
        for part in own:
            extra = part[VD:, :].astype(F32)
            logs.append(extra[0:1, :] + extra[1:2, :] + extra[2:3, :])
        best = jnp.maximum(jnp.maximum(logs[0], logs[1]), jnp.maximum(logs[2], logs[3]))
        shares = [jnp.exp(log - best) for log in logs]
        inverse = 1.0 / (shares[0] + shares[1] + shares[2] + shares[3])
        mixed = 0.0
        for part, share in zip(own, shares):
            mixed = mixed + part[:VD, :].astype(F32) * (share * inverse)
        heads.append(mixed)
    attention = jnp.concatenate(heads, axis=0).T.astype(BF16)
    scratch[...] = dot_nn(attention, weight_ref[...]).reshape(scratch.shape)
    send_ref[...] = scratch[:, 1 - core].reshape(send_ref.shape).astype(BF16)
    keep_ref[...] = scratch[:, core].reshape(keep_ref.shape)


def add_kernel(keep_ref, got_ref, out_ref):
    total = keep_ref[...] + got_ref[...].astype(F32)
    out_ref[...] = total.astype(BF16).reshape(out_ref.shape)


def hidden_kernel(parts_ref, residual_ref, ids_ref, weights_ref, hidden_ref, payload_ref):
    total = residual_ref[...].astype(F32)
    mixed = parts_ref[0].astype(F32)
    for index in range(1, parts_ref.shape[0]):
        mixed = mixed + parts_ref[index].astype(F32)
    hidden = (total + mixed).astype(BF16)
    hidden_ref[...] = hidden
    floats = hidden.astype(F32)
    squares = jnp.sum(floats * floats, axis=1, keepdims=True)
    top = ids_ref.shape[1]
    row, lane = iota((top, TAIL), 0), iota((top, TAIL), 1)
    tail = dot_nn(
        ids_ref[...].astype(F32).astype(BF16), jnp.where(lane == row, 1.0, 0.0).astype(BF16)
    )
    for index, piece in enumerate(split3(weights_ref[...])):
        where = lane == row + (index + 1) * top
        tail = tail + dot_nn(piece, jnp.where(where, 1.0, 0.0).astype(BF16))
    lane = iota((hidden.shape[0], TAIL), 1)
    for index, piece in enumerate(split3(squares)):
        tail = jnp.where(lane == 4 * top + index, piece.astype(F32), tail)
    tail = tail.astype(BF16)
    width = hidden.shape[1]
    for index in range(payload_ref.shape[0]):
        payload_ref[index, :, :width] = hidden
        payload_ref[index, :, width:] = tail


def select_kernel(place, own_ref, other_ref, low_ref, high_ref, pick_ref):
    expert = place[1].astype(F32)
    half = own_ref.shape[0]
    rows = 2 * half
    slots = pick_ref.shape[1]
    width = own_ref.shape[1] - TAIL
    tails = jnp.concatenate([own_ref[:, width:], other_ref[:, width:]], axis=0).astype(F32)
    lane = iota((rows, TAIL), 1)
    named = jnp.max(
        jnp.where((tails == expert) & (lane < 8), 1.0, 0.0), axis=1, keepdims=True
    )
    ahead = (iota((rows, rows), 1) < iota((rows, rows), 0)) & (
        iota((rows, rows), 1) // 8 == iota((rows, rows), 0) // 8
    )
    before = dot_nn(
        jnp.where(ahead, 1.0, 0.0).astype(BF16),
        jnp.broadcast_to(named, (rows, TAIL)).astype(BF16),
    )[:, :1]
    place_of = (iota((rows, 1), 0) // 8 * CAP).astype(F32) + before
    slot = iota((rows, slots), 1).astype(F32)
    pick = jnp.where((slot == place_of) & (named > 0.5), 1.0, 0.0)
    pick_ref[...] = pick.astype(BF16)
    turned = pick.T.astype(BF16)
    chosen = dot_nn(turned[:, :half], own_ref[...]) + dot_nn(turned[:, half:], other_ref[...])
    chosen = chosen.astype(BF16)
    low_ref[...] = chosen[: slots // 2]
    high_ref[...] = chosen[slots // 2 :]


def expert_kernel(place, *refs):
    context, expert = place[0], place[1].astype(F32)
    parts = refs[:8]
    gain_ref, gate_ref, up_ref, down_ref, own_ref = refs[8:13]
    sends = refs[13:]
    slots = own_ref.shape[0]
    width = own_ref.shape[1]
    count = 4
    lane = iota((slots, TAIL), 1)
    squares = 0.0
    for index in range(count):
        tail = jnp.concatenate([parts[2 * index][:, width:], parts[2 * index + 1][:, width:]], axis=0)
        tail = tail.astype(F32)
        squares = squares + jnp.sum(
            jnp.where((lane >= 32) & (lane < 35), tail, 0.0), axis=1, keepdims=True
        )
        if index == 0:
            shares = (
                pltpu.roll(tail, TAIL - 8, 1)
                + pltpu.roll(tail, TAIL - 16, 1)
                + pltpu.roll(tail, TAIL - 24, 1)
            )
            share = jnp.sum(
                jnp.where((tail == expert) & (lane < 8), shares, 0.0), axis=1, keepdims=True
            )
    inverse = lax.rsqrt(squares * (1.0 / (count * width)) + NORM_EPSILON)
    gate_part = jnp.zeros((slots, gate_ref.shape[1]), F32)
    up_part = gate_part
    for index in range(count):
        source = lax.rem(context + (count - index), count)
        rows = jnp.concatenate(
            [parts[2 * index][:, :width], parts[2 * index + 1][:, :width]], axis=0
        )
        normed = (rows.astype(F32) * inverse * gain_ref[source]).astype(BF16)
        at = pl.ds(pl.multiple_of(source * width, width), width)
        gate_part = gate_part + dot_nn(normed, gate_ref[at, :])
        up_part = up_part + dot_nn(normed, up_ref[at, :])
    active = (gate_part / (1.0 + jnp.exp(-gate_part)) * up_part).astype(BF16)
    for index in (2, 1, 3, 0):
        target = lax.rem(context + index, count)
        at = pl.ds(pl.multiple_of(target * width, 128), width)
        made = dot_nn(active, down_ref[:, at]) * share
        if index == 0:
            own_ref[...] = made
        else:
            made = made.astype(BF16)
            sends[2 * index - 2][...] = made[: slots // 2]
            sends[2 * index - 1][...] = made[slots // 2 :]


def spread_kernel(own_ref, low1, high1, low3, high3, pick_ref, send_ref, keep_ref):
    slots = own_ref.shape[0]
    half = slots // 2
    low = own_ref[:half] + low1[...].astype(F32) + low3[...].astype(F32)
    high = own_ref[half:] + high1[...].astype(F32) + high3[...].astype(F32)
    total = jnp.concatenate([low, high], axis=0).astype(BF16)
    rows = keep_ref.shape[0]
    keep_ref[...] = dot_nn(pick_ref[:rows, :], total)
    send_ref[...] = dot_nn(pick_ref[rows:, :], total).astype(BF16)


def call(kernel, outs, inputs, scalars=0, scratch=()):
    return pl.pallas_call(
        kernel,
        out_shape=tuple(jax.ShapeDtypeStruct(shape, dtype) for shape, dtype in outs),
        in_specs=[SMEM] * scalars + [VMEM] * (len(inputs) - scalars),
        out_specs=tuple(VMEM for _ in outs),
        scratch_shapes=list(scratch),
        name=kernel.__name__,
    )(*inputs)


def shift(value, axis, count, step):
    return lax.ppermute(value, axis, [(i, (i + step) % count) for i in range(count)])


def local(
    queries,
    key_lift,
    value_lift,
    page_pool,
    fresh_latents,
    page_table,
    context_lengths,
    tree_parents,
    out_weight,
    residual,
    norm_gain,
    expert_ids,
    route_weights,
    gate_matrix,
    up_matrix,
    down_matrix,
):
    rows = queries.shape[0]
    row_dev, width = residual.shape
    ring = lax.axis_size(CONTEXT)
    chips = lax.axis_size(ROW_AXES)
    half = rows // 2
    slots = rows // row_dev * CAP
    context = lax.axis_index(CONTEXT)
    expert = lax.axis_index(EXPERT)
    core = lax.axis_index(CORE)
    number = jnp.arange(4, dtype=jnp.int32)
    place = jnp.where(number == 0, context, jnp.where(number == 1, expert, core)).astype(jnp.int32)

    low, high = call(
        attention_kernel,
        [((VD + 16, rows), BF16)] * 2,
        [
            place,
            queries,
            key_lift,
            value_lift,
            page_pool.reshape(-1, page_pool.shape[-1]),
            fresh_latents.reshape(-1, fresh_latents.shape[-1]),
            page_table,
            context_lengths.reshape(1, -1),
            tree_parents,
        ],
        scalars=1,
    )

    def around(low, high):
        low1, high1 = shift(low, CONTEXT, ring, 1), shift(high, CONTEXT, ring, 1)
        low3, high3 = shift(low, CONTEXT, ring, -1), shift(high, CONTEXT, ring, -1)
        low2, high2 = shift(low1, CONTEXT, ring, 1), shift(high3, CONTEXT, ring, -1)
        return (low, low1, low2, low3), (high, high1, high2, high3)

    lows, highs = around(low, high)
    send, keep = call(
        merge_kernel,
        [((half, width), BF16), ((half, width), F32)],
        [place, *lows, *highs, out_weight],
        scalars=1,
        scratch=[pltpu.VMEM((chips, 2, row_dev, width), F32)],
    )

    def return_rows(send, keep):
        got = shift(send, CORE, 2, 1)
        (summed,) = call(add_kernel, [((chips, row_dev, width), BF16)], [keep, got])
        return lax.all_to_all(summed, ROW_AXES, 0, 0, tiled=True)

    mixed = return_rows(send, keep)
    hidden, payload = call(
        hidden_kernel,
        [((row_dev, width), BF16), ((chips, row_dev, width + TAIL), BF16)],
        [mixed, residual, expert_ids, route_weights],
    )
    own = lax.all_to_all(payload, ROW_AXES, 0, 0, tiled=True).reshape(half, width + TAIL)
    other = shift(own, CORE, 2, 1)
    low, high, pick = call(
        select_kernel,
        [((slots // 2, width + TAIL), BF16)] * 2 + [((rows, slots), BF16)],
        [place, own, other],
        scalars=1,
    )
    lows, highs = around(low, high)
    parts = [part for pair in zip(lows, highs) for part in pair]
    made, low1, high1, low2, high2, low3, high3 = call(
        expert_kernel,
        [((slots, width), F32)] + [((slots // 2, width), BF16)] * 6,
        [
            place,
            *parts,
            norm_gain.reshape(ring, 1, width),
            gate_matrix[0],
            up_matrix[0],
            down_matrix[0],
        ],
        scalars=1,
    )
    passed_low = shift(low2, CONTEXT, ring, 1)
    passed_high = shift(high2, CONTEXT, ring, -1)
    got_high1 = shift(high1, CONTEXT, ring, 1)
    got_low3 = shift(low3, CONTEXT, ring, -1)
    got_low1 = shift((low1.astype(F32) + passed_low.astype(F32)).astype(BF16), CONTEXT, ring, 1)
    got_high3 = shift((high3.astype(F32) + passed_high.astype(F32)).astype(BF16), CONTEXT, ring, -1)
    send, keep = call(
        spread_kernel,
        [((half, width), BF16), ((half, width), F32)],
        [made, got_low1, got_high1, got_low3, got_high3, pick],
    )
    returned = return_rows(send, keep)
    total = jnp.sum(returned.astype(F32), axis=0)
    return (hidden.astype(F32) + total).astype(BF16)


def solution(mesh):
    fine = Mesh(mesh.devices.reshape(4, 4, 8, 2), (CONTEXT, "x", "z", CORE))
    return jax.shard_map(
        local,
        mesh=fine,
        in_specs=(
            P(None, EXPERT),
            P(EXPERT, None, None),
            P(EXPERT, None, None),
            P(CONTEXT, None, None),
            P(CONTEXT, None, None),
            P(),
            P(),
            P(),
            P(EXPERT, CONTEXT),
            P(EXPERT, CONTEXT),
            P(),
            P(EXPERT, None),
            P(EXPERT, None),
            P(EXPERT, None, CONTEXT),
            P(EXPERT, None, CONTEXT),
            P(EXPERT, CONTEXT, None),
        ),
        out_specs=P(EXPERT, CONTEXT),
        check_vma=False,
    )
```

```python
import jax
import jax.numpy as jnp
from jax import lax
from jax.experimental import pallas as pl
from jax.experimental.pallas import tpu as pltpu
from jax.sharding import Mesh, PartitionSpec as P

LAT = 512
ROPE = 64
QK = 128
VD = 128
PAGE = 64
LOOK = 8
CAP = 3
NEGATIVE_FILL = -1e30
NORM_EPSILON = 1e-06
F32 = jnp.float32
BF16 = jnp.bfloat16
SMEM = pl.BlockSpec(memory_space=pltpu.SMEM)
VMEM = pl.BlockSpec(memory_space=pltpu.VMEM)
TAIL = 128

CONTEXT = "context"
ROW_AXES = ("x", "z")
CORE = "core"
EXPERT = ("x", "z", "core")


def iota(shape, axis):
    return lax.broadcasted_iota(jnp.int32, shape, axis)


def dot_nn(a, b):
    return jnp.dot(a, b, preferred_element_type=F32)


def dot_nt(a, b):
    return lax.dot_general(a, b, (((1,), (1,)), ((), ())), preferred_element_type=F32)


def dot_tn(a, b):
    return lax.dot_general(a, b, (((0,), (0,)), ((), ())), preferred_element_type=F32)


def split3(value):
    high = value.astype(BF16)
    rest = value - high.astype(F32)
    middle = rest.astype(BF16)
    low = (rest - middle.astype(F32)).astype(BF16)
    return high, middle, low


def attention_kernel(
    place, q_ref, kl_ref, vl_ref, pool_ref, fresh_ref, table_ref, length_ref, parent_ref, *outs
):
    context = place[0]
    pool_rows = pool_ref.shape[0]
    fresh_rows = fresh_ref.shape[0]
    rows = q_ref.shape[0]
    leaves, table_len = table_ref.shape
    pages = pool_rows // PAGE
    lengths = jnp.sum(
        jnp.where(
            iota((leaves, leaves), 0) == iota((leaves, leaves), 1),
            length_ref[...].astype(F32),
            0.0,
        ),
        axis=1,
        keepdims=True,
    )
    remain = lengths - (iota((leaves, table_len), 1) * PAGE).astype(F32)
    remain = jnp.clip(remain, 0.0, float(PAGE))
    table = table_ref[...]
    lane = iota((leaves, 128), 1)
    limits = jnp.zeros((leaves, 128), F32)
    for page in range(pages):
        seen = jnp.sum(
            jnp.where(table == context * pages + page, remain, 0.0), axis=1, keepdims=True
        )
        limits = jnp.where(lane == page, seen, limits)
    spread = (iota((leaves, rows), 0) == iota((leaves, rows), 1) // LOOK).astype(F32).astype(BF16)
    row_limits = dot_nn(limits.T.astype(BF16), spread)
    page_limit = jnp.concatenate(
        [jnp.broadcast_to(row_limits[p : p + 1, :], (PAGE, rows)) for p in range(pages)], axis=0
    )
    within = jnp.bitwise_and(iota((pool_rows, rows), 0), PAGE - 1).astype(F32)
    page_mask = jnp.where(within < page_limit, 1.0, 0.0)
    own_leaves = fresh_rows // LOOK
    pick_leaf = (
        (iota((fresh_rows, leaves), 1) == context * own_leaves + iota((fresh_rows, leaves), 0) // LOOK)
        .astype(F32)
        .astype(BF16)
    )
    parents = dot_nn(pick_leaf, parent_ref[...].astype(F32).astype(BF16))
    token = jnp.bitwise_and(iota((fresh_rows, LOOK), 0), LOOK - 1)
    parent = jnp.sum(
        jnp.where(iota((fresh_rows, LOOK), 1) == token, parents, 0.0), axis=1, keepdims=True
    )
    square = (fresh_rows, fresh_rows)
    first = (iota(square, 0) // LOOK) * LOOK
    step = (iota(square, 1) - first).astype(F32)
    linked = jnp.where((step == parent) & (parent >= 0.0), 1.0, 0.0)
    linked = jnp.where(iota(square, 0) == iota(square, 1), 1.0, linked)
    for repeat in range(3):
        half = linked.astype(BF16)
        linked = jnp.where(dot_nn(half, half) > 0.5, 1.0, 0.0)
    fresh_mask = jnp.concatenate([linked.T] * (rows // fresh_rows), axis=1)
    here = iota((fresh_rows, rows), 1) // fresh_rows == context
    fresh_mask = jnp.where(here, fresh_mask, 0.0)
    mask = jnp.concatenate([page_mask, fresh_mask], axis=0) > 0.5

    keys = jnp.concatenate([pool_ref[...], fresh_ref[...]], axis=0)
    latents = keys[:, :LAT]
    turned = keys[:, LAT:]
    scale = (QK + ROPE) ** (-0.5)
    for head, out in enumerate(outs):
        start = head * (QK + ROPE)
        plain = q_ref[:, start : start + QK]
        rotary = q_ref[:, start + QK : start + QK + ROPE]
        lifted = dot_nn(plain, kl_ref[head]).astype(BF16)
        scores = (dot_nt(latents, lifted) + dot_nt(turned, rotary)) * scale
        scores = jnp.where(mask, scores, NEGATIVE_FILL)
        best = jnp.max(scores, axis=0, keepdims=True)
        weights = jnp.exp(scores - best)
        total = jnp.sum(weights, axis=0, keepdims=True)
        values = dot_nn(latents, vl_ref[head]).T.astype(BF16)
        mixed = dot_nn(values, weights.astype(BF16)) / total
        out[:VD, :] = mixed.astype(BF16)
        high, middle, low = split3(best + jnp.log(total))
        line = iota((16, rows), 0)
        extra = jnp.where(
            line == 0,
            high.astype(F32),
            jnp.where(line == 1, middle.astype(F32), jnp.where(line == 2, low.astype(F32), 0.0)),
        )
        out[VD:, :] = extra.astype(BF16)


def merge_kernel(place, *refs):
    core = place[2]
    parts, (weight_ref, send_ref, keep_ref, scratch) = refs[:8], refs[8:]
    heads = []
    for head in range(2):
        own = parts[4 * head : 4 * head + 4]
        logs = []
        for part in own:
            extra = part[VD:, :].astype(F32)
            logs.append(extra[0:1, :] + extra[1:2, :] + extra[2:3, :])
        best = jnp.maximum(jnp.maximum(logs[0], logs[1]), jnp.maximum(logs[2], logs[3]))
        shares = [jnp.exp(log - best) for log in logs]
        inverse = 1.0 / (shares[0] + shares[1] + shares[2] + shares[3])
        mixed = 0.0
        for part, share in zip(own, shares):
            mixed = mixed + part[:VD, :].astype(F32) * (share * inverse)
        heads.append(mixed)
    attention = jnp.concatenate(heads, axis=0).T.astype(BF16)
    scratch[...] = dot_nn(attention, weight_ref[...]).reshape(scratch.shape)
    send_ref[...] = scratch[:, 1 - core].reshape(send_ref.shape).astype(BF16)
    keep_ref[...] = scratch[:, core].reshape(keep_ref.shape)


def add_kernel(keep_ref, got_ref, out_ref):
    total = keep_ref[...] + got_ref[...].astype(F32)
    out_ref[...] = total.astype(BF16).reshape(out_ref.shape)


def hidden_kernel(parts_ref, residual_ref, ids_ref, weights_ref, hidden_ref, payload_ref):
    total = residual_ref[...].astype(F32)
    mixed = parts_ref[0].astype(F32)
    for index in range(1, parts_ref.shape[0]):
        mixed = mixed + parts_ref[index].astype(F32)
    hidden = (total + mixed).astype(BF16)
    hidden_ref[...] = hidden
    floats = hidden.astype(F32)
    squares = jnp.sum(floats * floats, axis=1, keepdims=True)
    top = ids_ref.shape[1]
    row, lane = iota((top, TAIL), 0), iota((top, TAIL), 1)
    tail = dot_nn(
        ids_ref[...].astype(F32).astype(BF16), jnp.where(lane == row, 1.0, 0.0).astype(BF16)
    )
    for index, piece in enumerate(split3(weights_ref[...])):
        where = lane == row + (index + 1) * top
        tail = tail + dot_nn(piece, jnp.where(where, 1.0, 0.0).astype(BF16))
    lane = iota((hidden.shape[0], TAIL), 1)
    for index, piece in enumerate(split3(squares)):
        tail = jnp.where(lane == 4 * top + index, piece.astype(F32), tail)
    tail = tail.astype(BF16)
    width = hidden.shape[1]
    for index in range(payload_ref.shape[0]):
        payload_ref[index, :, :width] = hidden
        payload_ref[index, :, width:] = tail


def select_kernel(place, own_ref, other_ref, low_ref, high_ref, pick_ref):
    expert = place[1].astype(F32)
    half = own_ref.shape[0]
    rows = 2 * half
    slots = pick_ref.shape[1]
    width = own_ref.shape[1] - TAIL
    tails = jnp.concatenate([own_ref[:, width:], other_ref[:, width:]], axis=0).astype(F32)
    lane = iota((rows, TAIL), 1)
    named = jnp.max(
        jnp.where((tails == expert) & (lane < 8), 1.0, 0.0), axis=1, keepdims=True
    )
    ahead = (iota((rows, rows), 1) < iota((rows, rows), 0)) & (
        iota((rows, rows), 1) // 8 == iota((rows, rows), 0) // 8
    )
    before = dot_nn(
        jnp.where(ahead, 1.0, 0.0).astype(BF16),
        jnp.broadcast_to(named, (rows, TAIL)).astype(BF16),
    )[:, :1]
    place_of = (iota((rows, 1), 0) // 8 * CAP).astype(F32) + before
    slot = iota((rows, slots), 1).astype(F32)
    pick = jnp.where((slot == place_of) & (named > 0.5), 1.0, 0.0)
    pick_ref[...] = pick.astype(BF16)
    turned = pick.T.astype(BF16)
    chosen = dot_nn(turned[:, :half], own_ref[...]) + dot_nn(turned[:, half:], other_ref[...])
    chosen = chosen.astype(BF16)
    low_ref[...] = chosen[: slots // 2]
    high_ref[...] = chosen[slots // 2 :]


def expert_kernel(place, *refs):
    context, expert = place[0], place[1].astype(F32)
    parts = refs[:8]
    gain_ref, gate_ref, up_ref, down_ref, own_ref = refs[8:13]
    sends = refs[13:]
    slots = own_ref.shape[0]
    width = own_ref.shape[1]
    count = 4
    lane = iota((slots, TAIL), 1)
    squares = 0.0
    for index in range(count):
        tail = jnp.concatenate([parts[2 * index][:, width:], parts[2 * index + 1][:, width:]], axis=0)
        tail = tail.astype(F32)
        squares = squares + jnp.sum(
            jnp.where((lane >= 32) & (lane < 35), tail, 0.0), axis=1, keepdims=True
        )
        if index == 0:
            shares = (
                pltpu.roll(tail, TAIL - 8, 1)
                + pltpu.roll(tail, TAIL - 16, 1)
                + pltpu.roll(tail, TAIL - 24, 1)
            )
            share = jnp.sum(
                jnp.where((tail == expert) & (lane < 8), shares, 0.0), axis=1, keepdims=True
            )
    inverse = lax.rsqrt(squares * (1.0 / (count * width)) + NORM_EPSILON)
    gate_part = jnp.zeros((slots, gate_ref.shape[1]), F32)
    up_part = gate_part
    for index in range(count):
        source = lax.rem(context + (count - index), count)
        rows = jnp.concatenate(
            [parts[2 * index][:, :width], parts[2 * index + 1][:, :width]], axis=0
        )
        normed = (rows.astype(F32) * inverse * gain_ref[source]).astype(BF16)
        at = pl.ds(pl.multiple_of(source * width, width), width)
        gate_part = gate_part + dot_nn(normed, gate_ref[at, :])
        up_part = up_part + dot_nn(normed, up_ref[at, :])
    active = (gate_part / (1.0 + jnp.exp(-gate_part)) * up_part).astype(BF16)
    for index in (2, 1, 3, 0):
        target = lax.rem(context + index, count)
        at = pl.ds(pl.multiple_of(target * width, 128), width)
        made = dot_nn(active, down_ref[:, at]) * share
        if index == 0:
            own_ref[...] = made
        else:
            made = made.astype(BF16)
            sends[2 * index - 2][...] = made[: slots // 2]
            sends[2 * index - 1][...] = made[slots // 2 :]


def spread_kernel(own_ref, low1, high1, low3, high3, pick_ref, send_ref, keep_ref):
    slots = own_ref.shape[0]
    half = slots // 2
    low = own_ref[:half] + low1[...].astype(F32) + low3[...].astype(F32)
    high = own_ref[half:] + high1[...].astype(F32) + high3[...].astype(F32)
    total = jnp.concatenate([low, high], axis=0).astype(BF16)
    rows = keep_ref.shape[0]
    keep_ref[...] = dot_nn(pick_ref[:rows, :], total)
    send_ref[...] = dot_nn(pick_ref[rows:, :], total).astype(BF16)


def call(kernel, outs, inputs, scalars=0, scratch=(), limit=16, hold=True):
    held = inputs[scalars:]
    if hold:
        held = [pltpu.with_memory_space_constraint(value, pltpu.VMEM) for value in held]
    return pl.pallas_call(
        kernel,
        out_shape=tuple(pltpu.VMEM(shape, dtype) for shape, dtype in outs),
        in_specs=[SMEM] * scalars + [VMEM] * len(held),
        out_specs=tuple(VMEM for _ in outs),
        scratch_shapes=list(scratch),
        compiler_params=pltpu.CompilerParams(vmem_limit_bytes=limit << 20),
        name=kernel.__name__,
    )(*inputs[:scalars], *held)


def shift(value, axis, count, step):
    return lax.ppermute(value, axis, [(i, (i + step) % count) for i in range(count)])


def local(
    queries,
    key_lift,
    value_lift,
    page_pool,
    fresh_latents,
    page_table,
    context_lengths,
    tree_parents,
    out_weight,
    residual,
    norm_gain,
    expert_ids,
    route_weights,
    gate_matrix,
    up_matrix,
    down_matrix,
):
    rows = queries.shape[0]
    row_dev, width = residual.shape
    ring = lax.axis_size(CONTEXT)
    chips = lax.axis_size(ROW_AXES)
    half = rows // 2
    slots = rows // row_dev * CAP
    context = lax.axis_index(CONTEXT)
    expert = lax.axis_index(EXPERT)
    core = lax.axis_index(CORE)
    number = jnp.arange(4, dtype=jnp.int32)
    place = jnp.where(number == 0, context, jnp.where(number == 1, expert, core)).astype(jnp.int32)

    low, high = call(
        attention_kernel,
        [((VD + 16, rows), BF16)] * 2,
        [
            place,
            queries,
            key_lift,
            value_lift,
            page_pool.reshape(-1, page_pool.shape[-1]),
            fresh_latents.reshape(-1, fresh_latents.shape[-1]),
            page_table,
            context_lengths.reshape(1, -1),
            tree_parents,
        ],
        scalars=1,
        hold=False,
    )

    def around(low, high):
        low1, high1 = shift(low, CONTEXT, ring, 1), shift(high, CONTEXT, ring, 1)
        low3, high3 = shift(low, CONTEXT, ring, -1), shift(high, CONTEXT, ring, -1)
        low2, high2 = shift(low1, CONTEXT, ring, 1), shift(high3, CONTEXT, ring, -1)
        return (low, low1, low2, low3), (high, high1, high2, high3)

    lows, highs = around(low, high)
    send, keep = call(
        merge_kernel,
        [((half, width), BF16), ((half, width), F32)],
        [place, *lows, *highs, out_weight],
        scalars=1,
        scratch=[pltpu.VMEM((chips, 2, row_dev, width), F32)],
    )

    def return_rows(send, keep):
        got = shift(send, CORE, 2, 1)
        (summed,) = call(add_kernel, [((chips, row_dev, width), BF16)], [keep, got])
        return lax.all_to_all(summed, ROW_AXES, 0, 0, tiled=True)

    mixed = return_rows(send, keep)
    hidden, payload = call(
        hidden_kernel,
        [((row_dev, width), BF16), ((chips, row_dev, width + TAIL), BF16)],
        [mixed, residual, expert_ids, route_weights],
    )
    own = lax.all_to_all(payload, ROW_AXES, 0, 0, tiled=True).reshape(half, width + TAIL)
    other = shift(own, CORE, 2, 1)
    low, high, pick = call(
        select_kernel,
        [((slots // 2, width + TAIL), BF16)] * 2 + [((rows, slots), BF16)],
        [place, own, other],
        scalars=1,
    )
    lows, highs = around(low, high)
    parts = [part for pair in zip(lows, highs) for part in pair]
    made, low1, high1, low2, high2, low3, high3 = call(
        expert_kernel,
        [((slots, width), F32)] + [((slots // 2, width), BF16)] * 6,
        [
            place,
            *parts,
            norm_gain.reshape(ring, 1, width),
            gate_matrix[0],
            up_matrix[0],
            down_matrix[0],
        ],
        scalars=1,
    )
    passed_low = shift(low2, CONTEXT, ring, 1)
    passed_high = shift(high2, CONTEXT, ring, -1)
    got_high1 = shift(high1, CONTEXT, ring, 1)
    got_low3 = shift(low3, CONTEXT, ring, -1)
    got_low1 = shift((low1.astype(F32) + passed_low.astype(F32)).astype(BF16), CONTEXT, ring, 1)
    got_high3 = shift((high3.astype(F32) + passed_high.astype(F32)).astype(BF16), CONTEXT, ring, -1)
    send, keep = call(
        spread_kernel,
        [((half, width), BF16), ((half, width), F32)],
        [made, got_low1, got_high1, got_low3, got_high3, pick],
    )
    returned = return_rows(send, keep)
    total = jnp.sum(returned.astype(F32), axis=0)
    return (hidden.astype(F32) + total).astype(BF16)


def solution(mesh):
    fine = Mesh(mesh.devices.reshape(4, 4, 8, 2), (CONTEXT, "x", "z", CORE))
    return jax.shard_map(
        local,
        mesh=fine,
        in_specs=(
            P(None, EXPERT),
            P(EXPERT, None, None),
            P(EXPERT, None, None),
            P(CONTEXT, None, None),
            P(CONTEXT, None, None),
            P(),
            P(),
            P(),
            P(EXPERT, CONTEXT),
            P(EXPERT, CONTEXT),
            P(),
            P(EXPERT, None),
            P(EXPERT, None),
            P(EXPERT, None, CONTEXT),
            P(EXPERT, None, CONTEXT),
            P(EXPERT, CONTEXT, None),
        ),
        out_specs=P(EXPERT, CONTEXT),
        check_vma=False,
    )
```

```python
import jax
import jax.numpy as jnp
from jax import lax
from jax.experimental import pallas as pl
from jax.experimental.pallas import tpu as pltpu
from jax.sharding import Mesh, PartitionSpec as P


LAT = 512
ROPE = 64
QK = 128
VD = 128
PAGE = 64
LOOK = 8
CAP = 3
NEGATIVE_FILL = -1e30
NORM_EPSILON = 1e-06
F32 = jnp.float32
BF16 = jnp.bfloat16
SMEM = pl.BlockSpec(memory_space=pltpu.SMEM)
VMEM = pl.BlockSpec(memory_space=pltpu.VMEM)
TAIL = 128


CONTEXT = "context"
WIDE = "x"
DEEP = "z"
CORE = "core"
EXPERT = (WIDE, DEEP, CORE)


def iota(shape, axis):
    return lax.broadcasted_iota(jnp.int32, shape, axis)


def dot_nn(a, b):
    return jnp.dot(a, b, preferred_element_type=F32)


def dot_nt(a, b):
    return lax.dot_general(a, b, (((1,), (1,)), ((), ())), preferred_element_type=F32)


def split3(value):
    high = value.astype(BF16)
    rest = value - high.astype(F32)
    middle = rest.astype(BF16)
    low = (rest - middle.astype(F32)).astype(BF16)
    return high, middle, low


def attention_kernel(
    place, q_ref, kl_ref, vl_ref, pool_ref, fresh_ref, table_ref, length_ref, parent_ref, *outs
):
    context = place[0]
    pool_rows = pool_ref.shape[0]
    fresh_rows = fresh_ref.shape[0]
    rows = q_ref.shape[0]
    table_len, leaves = table_ref.shape
    pages = pool_rows // PAGE
    passed = (iota((table_len, leaves), 0) * PAGE).astype(F32)
    remain = jnp.clip(length_ref[...].astype(F32) - passed, 0.0, float(PAGE))
    table = table_ref[...]
    line = iota((16, leaves), 0)
    limits = jnp.zeros((16, leaves), F32)
    for page in range(pages):
        seen = jnp.sum(
            jnp.where(table == context * pages + page, remain, 0.0), axis=0, keepdims=True
        )
        limits = jnp.where(line == page, seen, limits)
    spread = (iota((leaves, rows), 0) == iota((leaves, rows), 1) // LOOK).astype(F32).astype(BF16)
    row_limits = dot_nn(limits.astype(BF16), spread)
    page_limit = jnp.concatenate(
        [jnp.broadcast_to(row_limits[p : p + 1, :], (PAGE, rows)) for p in range(pages)], axis=0
    )
    within = jnp.bitwise_and(iota((pool_rows, rows), 0), PAGE - 1).astype(F32)
    page_mask = jnp.where(within < page_limit, 1.0, 0.0)
    own_leaves = fresh_rows // LOOK
    pick_leaf = (
        (iota((fresh_rows, leaves), 1) == context * own_leaves + iota((fresh_rows, leaves), 0) // LOOK)
        .astype(F32)
        .astype(BF16)
    )
    parents = dot_nt(pick_leaf, parent_ref[...].astype(F32).astype(BF16))
    token = jnp.bitwise_and(iota((fresh_rows, LOOK), 0), LOOK - 1)
    parent = jnp.sum(
        jnp.where(iota((fresh_rows, LOOK), 1) == token, parents, 0.0), axis=1, keepdims=True
    )
    square = (fresh_rows, fresh_rows)
    first = (iota(square, 0) // LOOK) * LOOK
    step = (iota(square, 1) - first).astype(F32)
    linked = jnp.where((step == parent) & (parent >= 0.0), 1.0, 0.0)
    linked = jnp.where(iota(square, 0) == iota(square, 1), 1.0, linked)
    for _ in range(3):
        half = linked.astype(BF16)
        linked = jnp.where(dot_nn(half, half) > 0.5, 1.0, 0.0)
    fresh_mask = jnp.concatenate([linked.T] * (rows // fresh_rows), axis=1)
    here = iota((fresh_rows, rows), 1) // fresh_rows == context
    fresh_mask = jnp.where(here, fresh_mask, 0.0)
    mask = jnp.concatenate([page_mask, fresh_mask], axis=0) > 0.5

    keys = jnp.concatenate([pool_ref[...], fresh_ref[...]], axis=0)
    latents = keys[:, :LAT]
    turned = keys[:, LAT:]
    scale = (QK + ROPE) ** (-0.5)
    for head, out in enumerate(outs):
        start = head * (QK + ROPE)
        plain = q_ref[:, start : start + QK]
        rotary = q_ref[:, start + QK : start + QK + ROPE]
        lifted = dot_nn(plain, kl_ref[head]).astype(BF16)
        scores = (dot_nt(latents, lifted) + dot_nt(turned, rotary)) * scale
        scores = jnp.where(mask, scores, NEGATIVE_FILL)
        best = jnp.max(scores, axis=0, keepdims=True)
        weights = jnp.exp(scores - best)
        total = jnp.sum(weights, axis=0, keepdims=True)
        values = dot_nn(latents, vl_ref[head]).T.astype(BF16)
        mixed = dot_nn(values, weights.astype(BF16)) / total
        out[:VD, :] = mixed.astype(BF16)
        high, middle, low = split3(best + jnp.log(total))
        line = iota((16, rows), 0)
        extra = jnp.where(
            line == 0,
            high.astype(F32),
            jnp.where(line == 1, middle.astype(F32), jnp.where(line == 2, low.astype(F32), 0.0)),
        )
        out[VD:, :] = extra.astype(BF16)


def merge_kernel(place, *refs):
    core = place[2]
    parts, (weight_ref, send_ref, keep_ref, scratch) = refs[:8], refs[8:]
    heads = []
    for head in range(2):
        own = parts[4 * head : 4 * head + 4]
        logs = []
        for part in own:
            extra = part[VD:, :].astype(F32)
            logs.append(extra[0:1, :] + extra[1:2, :] + extra[2:3, :])
        best = jnp.maximum(jnp.maximum(logs[0], logs[1]), jnp.maximum(logs[2], logs[3]))
        shares = [jnp.exp(log - best) for log in logs]
        inverse = 1.0 / (shares[0] + shares[1] + shares[2] + shares[3])
        mixed = 0.0
        for part, share in zip(own, shares):
            mixed = mixed + part[:VD, :].astype(F32) * (share * inverse)
        heads.append(mixed)
    attention = jnp.concatenate(heads, axis=0).T.astype(BF16)
    scratch[...] = dot_nn(attention, weight_ref[...]).reshape(scratch.shape)
    send_ref[...] = scratch[:, 1 - core].reshape(send_ref.shape).astype(BF16)
    keep_ref[...] = scratch[:, core].reshape(keep_ref.shape)


def add_kernel(place, keep_ref, got_ref, own_ref, *sends):
    rows = own_ref.shape[0]
    count = len(sends) + 1
    for step in range(count):
        target = lax.rem(place[3] + step, count)
        at = pl.ds(pl.multiple_of(target * rows, rows), rows)
        total = keep_ref[at, :] + got_ref[at, :].astype(F32)
        if step == 0:
            own_ref[...] = total
        else:
            sends[step - 1][...] = total.astype(BF16)


def sum_kernel(own_ref, *refs):
    total = own_ref[...]
    for ref in refs[:-1]:
        total = total + ref[...].astype(F32)
    refs[-1][...] = total.astype(BF16).reshape(refs[-1].shape)


def cut_kernel(place, down_ref, after_ref, *outs):
    width = outs[0].shape[1]
    count = len(outs) + 1
    for step, out in enumerate(outs, 1):
        target = lax.rem(place[0] + step, count)
        out[...] = down_ref[:, pl.ds(pl.multiple_of(target * width, 128), width)]


def hidden_kernel(parts_ref, residual_ref, ids_ref, weights_ref, hidden_ref, payload_ref):
    total = residual_ref[...].astype(F32)
    mixed = parts_ref[0].astype(F32)
    for index in range(1, parts_ref.shape[0]):
        mixed = mixed + parts_ref[index].astype(F32)
    hidden = (total + mixed).astype(BF16)
    hidden_ref[...] = hidden
    floats = hidden.astype(F32)
    squares = jnp.sum(floats * floats, axis=1, keepdims=True)
    top = ids_ref.shape[1]
    row, lane = iota((top, TAIL), 0), iota((top, TAIL), 1)
    tail = dot_nn(
        ids_ref[...].astype(F32).astype(BF16), jnp.where(lane == row, 1.0, 0.0).astype(BF16)
    )
    for index, piece in enumerate(split3(weights_ref[...])):
        where = lane == row + (index + 1) * top
        tail = tail + dot_nn(piece, jnp.where(where, 1.0, 0.0).astype(BF16))
    lane = iota((hidden.shape[0], TAIL), 1)
    for index, piece in enumerate(split3(squares)):
        tail = jnp.where(lane == 4 * top + index, piece.astype(F32), tail)
    tail = tail.astype(BF16)
    width = hidden.shape[1]
    for index in range(payload_ref.shape[0]):
        payload_ref[index, :, :width] = hidden
        payload_ref[index, :, width:] = tail


def select_kernel(place, *refs):
    parts, (low_ref, send_ref, pick_ref, other_ref) = refs[:4], refs[4:]
    rows, slots = pick_ref.shape
    values = jnp.concatenate([part[...] for part in parts], axis=0)
    width = values.shape[1] - TAIL
    tails = values[:, width:].astype(F32)
    lane = iota((rows, TAIL), 1)
    ahead = (iota((rows, rows), 1) < iota((rows, rows), 0)) & (
        iota((rows, rows), 1) // 8 == iota((rows, rows), 0) // 8
    )
    ahead = jnp.where(ahead, 1.0, 0.0).astype(BF16)
    first = (iota((rows, 1), 0) // 8 * CAP).astype(F32)
    slot = iota((rows, slots), 1).astype(F32)
    partner = place[1] + 1 - 2 * place[2]
    for expert, out, keep in ((place[1], low_ref, pick_ref), (partner, send_ref, other_ref)):
        named = jnp.max(
            jnp.where((tails == expert.astype(F32)) & (lane < 8), 1.0, 0.0), axis=1, keepdims=True
        )
        before = dot_nn(ahead, jnp.broadcast_to(named, (rows, TAIL)).astype(BF16))[:, :1]
        pick = jnp.where((slot == first + before) & (named > 0.5), 1.0, 0.0)
        keep[...] = pick.astype(BF16)
        out[...] = dot_nn(pick.T.astype(BF16), values).astype(BF16)


def expert_kernel(place, *refs):
    context, expert = place[0], place[1].astype(F32)
    parts = refs[:8]
    gain_ref, gate_ref, up_ref, active_ref, share_ref = refs[8:]
    slots = active_ref.shape[0]
    width = gain_ref.shape[2]
    count = 4
    lane = iota((slots, TAIL), 1)
    squares = 0.0
    for index in range(count):
        tail = jnp.concatenate([parts[2 * index][:, width:], parts[2 * index + 1][:, width:]], axis=0)
        tail = tail.astype(F32)
        squares = squares + jnp.sum(
            jnp.where((lane >= 32) & (lane < 35), tail, 0.0), axis=1, keepdims=True
        )
        if index == 0:
            shares = (
                pltpu.roll(tail, TAIL - 8, 1)
                + pltpu.roll(tail, TAIL - 16, 1)
                + pltpu.roll(tail, TAIL - 24, 1)
            )
            share = jnp.sum(
                jnp.where((tail == expert) & (lane < 8), shares, 0.0), axis=1, keepdims=True
            )
            share_ref[...] = jnp.broadcast_to(share, share_ref.shape)
    inverse = lax.rsqrt(squares * (1.0 / (count * width)) + NORM_EPSILON)
    gate_part = jnp.zeros((slots, gate_ref.shape[1]), F32)
    up_part = gate_part
    for index in range(count):
        source = lax.rem(context + (count - index), count)
        rows = jnp.concatenate(
            [parts[2 * index][:, :width], parts[2 * index + 1][:, :width]], axis=0
        )
        normed = (rows.astype(F32) * inverse * gain_ref[source]).astype(BF16)
        at = pl.ds(pl.multiple_of(source * width, width), width)
        gate_part = gate_part + dot_nn(normed, gate_ref[at, :])
        up_part = up_part + dot_nn(normed, up_ref[at, :])
    active_ref[...] = (gate_part / (1.0 + jnp.exp(-gate_part)) * up_part).astype(BF16)


def down_kernel(place, *refs):
    actives, others, (down_ref, share_ref, low_ref, high_ref) = refs[:4], refs[4:7], refs[7:]
    width = low_ref.shape[1]
    half = low_ref.shape[0]
    at = pl.ds(pl.multiple_of(place[0] * width, 128), width)
    made = dot_nn(actives[0][...], down_ref[:, at])
    for active, other in zip(actives[1:], others):
        made = made + dot_nn(active[...], other[...])
    made = (made * share_ref[:, :1]).astype(BF16)
    low_ref[...] = made[:half]
    high_ref[...] = made[half:]


def spread_kernel(low_ref, got_ref, pick_ref, other_ref, own_ref, *sends):
    rows = own_ref.shape[0]
    total = dot_nn(pick_ref[...], low_ref[...]) + dot_nn(other_ref[...], got_ref[...])
    own_ref[...] = total[:rows]
    for step, send in enumerate(sends, 1):
        send[...] = total[step * rows : (step + 1) * rows].astype(BF16)


def call(kernel, outs, inputs, scalars=0, scratch=(), limit=16, hold=True):
    held = inputs[scalars:]
    if hold:
        held = [pltpu.with_memory_space_constraint(value, pltpu.VMEM) for value in held]
    return pl.pallas_call(
        kernel,
        out_shape=tuple(pltpu.VMEM(shape, dtype) for shape, dtype in outs),
        in_specs=[SMEM] * scalars + [VMEM] * len(held),
        out_specs=tuple(VMEM for _ in outs),
        scratch_shapes=list(scratch),
        compiler_params=pltpu.CompilerParams(vmem_limit_bytes=limit << 20),
    )(*inputs[:scalars], *held)


def shift(value, axis, count, step):
    return lax.ppermute(value, axis, [(i, (i + step) % count) for i in range(count)])


def local(
    queries,
    key_lift,
    value_lift,
    page_pool,
    fresh_latents,
    page_table,
    context_lengths,
    tree_parents,
    out_weight,
    residual,
    norm_gain,
    expert_ids,
    route_weights,
    gate_matrix,
    up_matrix,
    down_matrix,
):
    rows = queries.shape[0]
    row_dev, width = residual.shape
    ring, wide, deep = lax.axis_size(CONTEXT), lax.axis_size(WIDE), lax.axis_size(DEEP)
    half = rows // 2
    slots = rows // row_dev * CAP
    full = width + TAIL
    hidden_units = gate_matrix.shape[2]
    expert = lax.axis_index(EXPERT)
    places = (lax.axis_index(CONTEXT), expert, lax.axis_index(CORE), lax.axis_index(WIDE))
    number = jnp.arange(4, dtype=jnp.int32)
    place = jnp.zeros((4,), jnp.int32)
    for index, value in enumerate(places):
        place = jnp.where(number == index, value, place)

    low, high = call(
        attention_kernel,
        [((VD + 16, rows), BF16)] * 2,
        [
            place,
            queries,
            key_lift,
            value_lift,
            page_pool.reshape(-1, page_pool.shape[-1]),
            fresh_latents.reshape(-1, fresh_latents.shape[-1]),
            page_table.T,
            context_lengths.reshape(1, -1),
            tree_parents.T,
        ],
        scalars=1,
        hold=False,
        limit=56,
    )

    def around(low, high):
        low1, high1 = shift(low, CONTEXT, ring, 1), shift(high, CONTEXT, ring, 1)
        low3, high3 = shift(low, CONTEXT, ring, -1), shift(high, CONTEXT, ring, -1)
        low2, high2 = shift(low1, CONTEXT, ring, 1), shift(high3, CONTEXT, ring, -1)
        return (low, low1, low2, low3), (high, high1, high2, high3)

    def gather(own, sends):
        chunk = [((deep, row_dev, width), BF16)]
        (summed,) = call(sum_kernel, chunk, [own, *sends])
        return lax.all_to_all(summed, DEEP, 0, 0, tiled=True)

    lows, highs = around(low, high)
    send, keep = call(
        merge_kernel,
        [((half, width), BF16), ((half, width), F32)],
        [place, *lows, *highs, out_weight],
        scalars=1,
        scratch=[pltpu.VMEM((wide * deep, 2, row_dev, width), F32)],
    )
    cuts = call(
        cut_kernel,
        [((hidden_units, width), BF16)] * (ring - 1),
        [place, down_matrix[0], send],
        scalars=1,
    )
    others = []
    for step, cut in enumerate(cuts, 1):
        others.append(shift(cut, CONTEXT, ring, step))
    split = [((half // wide, width), F32)] + [((half // wide, width), BF16)] * (wide - 1)
    got = shift(send, CORE, 2, 1)
    own, *sends = call(add_kernel, split, [place, keep, got], scalars=1)
    mixed = gather(own, [shift(part, WIDE, wide, step) for step, part in enumerate(sends, 1)])
    hidden, payload = call(
        hidden_kernel,
        [((row_dev, width), BF16), ((deep, row_dev, full), BF16)],
        [mixed, residual, expert_ids, route_weights],
    )
    near = lax.all_to_all(payload, DEEP, 0, 0, tiled=True).reshape(deep * row_dev, full)
    parts = [near] + [shift(near, WIDE, wide, step) for step in range(1, wide)]
    low, send, pick, pick_other = call(
        select_kernel,
        [((slots // 2, full), BF16)] * 2 + [((half, slots // 2), BF16)] * 2,
        [place, *parts],
        scalars=1,
    )
    lows, highs = around(low, shift(send, CORE, 2, 1))
    active, share = call(
        expert_kernel,
        [((slots, hidden_units), BF16), ((slots, TAIL), F32)],
        [
            place,
            *[part for pair in zip(lows, highs) for part in pair],
            norm_gain.reshape(ring, 1, width),
            gate_matrix[0],
            up_matrix[0],
        ],
        scalars=1,
    )
    actives = [active] + [shift(active, CONTEXT, ring, step) for step in range(1, ring)]
    low, high = call(
        down_kernel,
        [((slots // 2, width), BF16)] * 2,
        [place, *actives, *others, down_matrix[0], share],
        scalars=1,
    )
    own, *sends = call(
        spread_kernel, split, [low, shift(high, CORE, 2, 1), pick, pick_other]
    )
    returned = gather(own, [shift(part, WIDE, wide, -step) for step, part in enumerate(sends, 1)])
    total = jnp.sum(returned.astype(F32), axis=0)
    return (hidden.astype(F32) + total).astype(BF16)


def solution(mesh):
    fine = Mesh(mesh.devices.reshape(4, 4, 8, 2), (CONTEXT, WIDE, DEEP, CORE))
    return jax.shard_map(
        local,
        mesh=fine,
        in_specs=(
            P(None, EXPERT),
            P(EXPERT, None, None),
            P(EXPERT, None, None),
            P(CONTEXT, None, None),
            P(CONTEXT, None, None),
            P(),
            P(),
            P(),
            P(EXPERT, CONTEXT),
            P(EXPERT, CONTEXT),
            P(),
            P(EXPERT, None),
            P(EXPERT, None),
            P(EXPERT, None, CONTEXT),
            P(EXPERT, None, CONTEXT),
            P(EXPERT, CONTEXT, None),
        ),
        out_specs=P(EXPERT, CONTEXT),
        check_vma=False,
    )
```

```python
import jax
import jax.numpy as jnp
from jax import lax
from jax.experimental import pallas as pl
from jax.experimental.pallas import tpu as pltpu
from jax.sharding import Mesh, PartitionSpec as P


LAT = 512
ROPE = 64
QK = 128
VD = 128
PAGE = 64
LOOK = 8
CAP = 3
NEGATIVE_FILL = -1e30
NORM_EPSILON = 1e-06
F32 = jnp.float32
BF16 = jnp.bfloat16
SMEM = pl.BlockSpec(memory_space=pltpu.SMEM)
VMEM = pl.BlockSpec(memory_space=pltpu.VMEM)
TAIL = 128


CONTEXT = "context"
WIDE = "x"
DEEP = "z"
CORE = "core"
EXPERT = (WIDE, DEEP, CORE)


def iota(shape, axis):
    return lax.broadcasted_iota(jnp.int32, shape, axis)


def dot_nn(a, b):
    return jnp.dot(a, b, preferred_element_type=F32)


def dot_nt(a, b):
    return lax.dot_general(a, b, (((1,), (1,)), ((), ())), preferred_element_type=F32)


def split3(value):
    high = value.astype(BF16)
    rest = value - high.astype(F32)
    middle = rest.astype(BF16)
    low = (rest - middle.astype(F32)).astype(BF16)
    return high, middle, low


def attention_kernel(
    place, q_ref, kl_ref, vl_ref, pool_ref, fresh_ref, table_ref, length_ref, parent_ref, *outs
):
    context = place[0]
    pool_rows = pool_ref.shape[0]
    fresh_rows = fresh_ref.shape[0]
    rows = q_ref.shape[0]
    table_len, leaves = table_ref.shape
    pages = pool_rows // PAGE
    passed = (iota((table_len, leaves), 0) * PAGE).astype(F32)
    remain = jnp.clip(length_ref[...].astype(F32) - passed, 0.0, float(PAGE))
    table = table_ref[...]
    line = iota((16, leaves), 0)
    limits = jnp.zeros((16, leaves), F32)
    for page in range(pages):
        seen = jnp.sum(
            jnp.where(table == context * pages + page, remain, 0.0), axis=0, keepdims=True
        )
        limits = jnp.where(line == page, seen, limits)
    spread = (iota((leaves, rows), 0) == iota((leaves, rows), 1) // LOOK).astype(F32).astype(BF16)
    row_limits = dot_nn(limits.astype(BF16), spread)
    page_limit = jnp.concatenate(
        [jnp.broadcast_to(row_limits[p : p + 1, :], (PAGE, rows)) for p in range(pages)], axis=0
    )
    within = jnp.bitwise_and(iota((pool_rows, rows), 0), PAGE - 1).astype(F32)
    page_mask = jnp.where(within < page_limit, 1.0, 0.0)
    own_leaves = fresh_rows // LOOK
    pick_leaf = (
        (iota((fresh_rows, leaves), 1) == context * own_leaves + iota((fresh_rows, leaves), 0) // LOOK)
        .astype(F32)
        .astype(BF16)
    )
    parents = dot_nt(pick_leaf, parent_ref[...].astype(F32).astype(BF16))
    token = jnp.bitwise_and(iota((fresh_rows, LOOK), 0), LOOK - 1)
    parent = jnp.sum(
        jnp.where(iota((fresh_rows, LOOK), 1) == token, parents, 0.0), axis=1, keepdims=True
    )
    square = (fresh_rows, fresh_rows)
    first = (iota(square, 0) // LOOK) * LOOK
    step = (iota(square, 1) - first).astype(F32)
    linked = jnp.where((step == parent) & (parent >= 0.0), 1.0, 0.0)
    linked = jnp.where(iota(square, 0) == iota(square, 1), 1.0, linked)
    for _ in range(3):
        half = linked.astype(BF16)
        linked = jnp.where(dot_nn(half, half) > 0.5, 1.0, 0.0)
    fresh_mask = jnp.concatenate([linked.T] * (rows // fresh_rows), axis=1)
    here = iota((fresh_rows, rows), 1) // fresh_rows == context
    fresh_mask = jnp.where(here, fresh_mask, 0.0)
    mask = jnp.concatenate([page_mask, fresh_mask], axis=0) > 0.5

    keys = jnp.concatenate([pool_ref[...], fresh_ref[...]], axis=0)
    latents = keys[:, :LAT]
    turned = keys[:, LAT:]
    scale = (QK + ROPE) ** (-0.5)
    for head, out in enumerate(outs):
        start = head * (QK + ROPE)
        plain = q_ref[:, start : start + QK]
        rotary = q_ref[:, start + QK : start + QK + ROPE]
        lifted = dot_nn(plain, kl_ref[head]).astype(BF16)
        scores = (dot_nt(latents, lifted) + dot_nt(turned, rotary)) * scale
        scores = jnp.where(mask, scores, NEGATIVE_FILL)
        best = jnp.max(scores, axis=0, keepdims=True)
        weights = jnp.exp(scores - best)
        total = jnp.sum(weights, axis=0, keepdims=True)
        values = dot_nn(latents, vl_ref[head]).T.astype(BF16)
        mixed = dot_nn(values, weights.astype(BF16)) / total
        out[:VD, :] = mixed.astype(BF16)
        high, middle, low = split3(best + jnp.log(total))
        line = iota((16, rows), 0)
        extra = jnp.where(
            line == 0,
            high.astype(F32),
            jnp.where(line == 1, middle.astype(F32), jnp.where(line == 2, low.astype(F32), 0.0)),
        )
        out[VD:, :] = extra.astype(BF16)


def merge_kernel(place, *refs):
    core = place[2]
    parts, (weight_ref, send_ref, keep_ref, scratch, weight, done) = refs[:8], refs[8:]
    load = pltpu.make_async_copy(weight_ref, weight, done)
    load.start()
    heads = []
    for head in range(2):
        own = parts[4 * head : 4 * head + 4]
        logs = []
        for part in own:
            extra = part[VD:, :].astype(F32)
            logs.append(extra[0:1, :] + extra[1:2, :] + extra[2:3, :])
        best = jnp.maximum(jnp.maximum(logs[0], logs[1]), jnp.maximum(logs[2], logs[3]))
        shares = [jnp.exp(log - best) for log in logs]
        inverse = 1.0 / (shares[0] + shares[1] + shares[2] + shares[3])
        mixed = 0.0
        for part, share in zip(own, shares):
            mixed = mixed + part[:VD, :].astype(F32) * (share * inverse)
        heads.append(mixed)
    attention = jnp.concatenate(heads, axis=0).T.astype(BF16)
    load.wait()
    scratch[...] = dot_nn(attention, weight[...]).reshape(scratch.shape)
    send_ref[...] = scratch[:, 1 - core].reshape(send_ref.shape).astype(BF16)
    keep_ref[...] = scratch[:, core].reshape(keep_ref.shape)


def add_kernel(place, keep_ref, got_ref, own_ref, *sends):
    rows = own_ref.shape[0]
    count = len(sends) + 1
    for step in range(count):
        target = lax.rem(place[3] + step, count)
        at = pl.ds(pl.multiple_of(target * rows, rows), rows)
        total = keep_ref[at, :] + got_ref[at, :].astype(F32)
        if step == 0:
            own_ref[...] = total
        else:
            sends[step - 1][...] = total.astype(BF16)


def sum_kernel(own_ref, *refs):
    total = own_ref[...]
    for ref in refs[:-1]:
        total = total + ref[...].astype(F32)
    refs[-1][...] = total.astype(BF16).reshape(refs[-1].shape)


def cut_kernel(place, down_ref, after_ref, *outs):
    width = outs[0].shape[1]
    count = len(outs) + 1
    for step, out in enumerate(outs, 1):
        target = lax.rem(place[0] + step, count)
        out[...] = down_ref[:, pl.ds(pl.multiple_of(target * width, 128), width)]


def hidden_kernel(parts_ref, residual_ref, ids_ref, weights_ref, hidden_ref, payload_ref):
    total = residual_ref[...].astype(F32)
    mixed = parts_ref[0].astype(F32)
    for index in range(1, parts_ref.shape[0]):
        mixed = mixed + parts_ref[index].astype(F32)
    hidden = (total + mixed).astype(BF16)
    hidden_ref[...] = hidden
    floats = hidden.astype(F32)
    squares = jnp.sum(floats * floats, axis=1, keepdims=True)
    top = ids_ref.shape[1]
    row, lane = iota((top, TAIL), 0), iota((top, TAIL), 1)
    tail = dot_nn(
        ids_ref[...].astype(F32).astype(BF16), jnp.where(lane == row, 1.0, 0.0).astype(BF16)
    )
    for index, piece in enumerate(split3(weights_ref[...])):
        where = lane == row + (index + 1) * top
        tail = tail + dot_nn(piece, jnp.where(where, 1.0, 0.0).astype(BF16))
    lane = iota((hidden.shape[0], TAIL), 1)
    for index, piece in enumerate(split3(squares)):
        tail = jnp.where(lane == 4 * top + index, piece.astype(F32), tail)
    tail = tail.astype(BF16)
    width = hidden.shape[1]
    for index in range(payload_ref.shape[0]):
        payload_ref[index, :, :width] = hidden
        payload_ref[index, :, width:] = tail


def select_kernel(place, rows_ref, pick_ref, *outs):
    rows = rows_ref.shape[0]
    count = len(outs)
    slots = pick_ref.shape[1] // (2 * count)
    values = rows_ref[...]
    width = values.shape[1] - TAIL
    tails = values[:, width:].astype(F32)
    lane = iota((rows, TAIL), 1)
    base = place[1] - place[3] * place[4]
    named = jnp.zeros((rows, TAIL), F32)
    for index in range(2 * count):
        expert = lax.rem(place[3] + index // 2, count) * place[4] + base
        if index % 2:
            expert = expert + 1 - 2 * place[2]
        found = jnp.max(
            jnp.where((tails == expert.astype(F32)) & (lane < 8), 1.0, 0.0), axis=1, keepdims=True
        )
        named = jnp.where(lane == index, found, named)
    ahead = (iota((rows, rows), 1) < iota((rows, rows), 0)) & (
        iota((rows, rows), 1) // 8 == iota((rows, rows), 0) // 8
    )
    before = dot_nn(jnp.where(ahead, 1.0, 0.0).astype(BF16), named.astype(BF16))
    slot_of = before + (iota((rows, TAIL), 0) // 8 * CAP).astype(F32)
    slot = iota((rows, pick_ref.shape[1]), 1).astype(F32)
    pick = jnp.zeros((rows, pick_ref.shape[1]), F32)
    for index in range(2 * count):
        match = slot == slot_of[:, index : index + 1] + float(index * slots)
        pick = jnp.where(match & (named[:, index : index + 1] > 0.5), 1.0, pick)
    pick_ref[...] = pick.astype(BF16)
    chosen = dot_nn(pick.T.astype(BF16), values).astype(BF16)
    for step, out in enumerate(outs):
        out[...] = chosen[2 * slots * step : 2 * slots * (step + 1)]


def sort_kernel(*refs):
    parts, (low_ref, send_ref) = refs[:-2], refs[-2:]
    slots = parts[0].shape[0] // 2
    for step, part in enumerate(parts):
        low_ref[step * slots : (step + 1) * slots, :] = part[:slots, :]
        send_ref[step * slots : (step + 1) * slots, :] = part[slots:, :]


def back_kernel(low_ref, got_ref, *outs):
    slots = outs[0].shape[0] // 2
    for step, out in enumerate(outs):
        out[:slots, :] = low_ref[step * slots : (step + 1) * slots, :]
        out[slots:, :] = got_ref[step * slots : (step + 1) * slots, :]


def expert_kernel(place, *refs):
    context, expert = place[0], place[1].astype(F32)
    parts = refs[:8]
    gain_ref, gate_ref, up_ref, active_ref, share_ref = refs[8:]
    slots = active_ref.shape[0]
    width = gain_ref.shape[2]
    count = 4
    lane = iota((slots, TAIL), 1)
    squares = 0.0
    for index in range(count):
        tail = jnp.concatenate([parts[2 * index][:, width:], parts[2 * index + 1][:, width:]], axis=0)
        tail = tail.astype(F32)
        squares = squares + jnp.sum(
            jnp.where((lane >= 32) & (lane < 35), tail, 0.0), axis=1, keepdims=True
        )
        if index == 0:
            shares = (
                pltpu.roll(tail, TAIL - 8, 1)
                + pltpu.roll(tail, TAIL - 16, 1)
                + pltpu.roll(tail, TAIL - 24, 1)
            )
            share = jnp.sum(
                jnp.where((tail == expert) & (lane < 8), shares, 0.0), axis=1, keepdims=True
            )
            share_ref[...] = jnp.broadcast_to(share, share_ref.shape)
    inverse = lax.rsqrt(squares * (1.0 / (count * width)) + NORM_EPSILON)
    gate_part = jnp.zeros((slots, gate_ref.shape[1]), F32)
    up_part = gate_part
    for index in range(count):
        source = lax.rem(context + (count - index), count)
        rows = jnp.concatenate(
            [parts[2 * index][:, :width], parts[2 * index + 1][:, :width]], axis=0
        )
        normed = (rows.astype(F32) * inverse * gain_ref[source]).astype(BF16)
        at = pl.ds(pl.multiple_of(source * width, width), width)
        gate_part = gate_part + dot_nn(normed, gate_ref[at, :])
        up_part = up_part + dot_nn(normed, up_ref[at, :])
    active_ref[...] = (gate_part / (1.0 + jnp.exp(-gate_part)) * up_part).astype(BF16)


def down_kernel(place, *refs):
    actives, others, (down_ref, share_ref, low_ref, high_ref) = refs[:4], refs[4:7], refs[7:]
    width = low_ref.shape[1]
    half = low_ref.shape[0]
    at = pl.ds(pl.multiple_of(place[0] * width, 128), width)
    made = dot_nn(actives[0][...], down_ref[:, at])
    for active, other in zip(actives[1:], others):
        made = made + dot_nn(active[...], other[...])
    made = (made * share_ref[:, :1]).astype(BF16)
    low_ref[...] = made[:half]
    high_ref[...] = made[half:]


def spread_kernel(pick_ref, *refs):
    values = jnp.concatenate([ref[...] for ref in refs[:-1]], axis=0)
    refs[-1][...] = dot_nn(pick_ref[...], values).astype(BF16).reshape(refs[-1].shape)


def output_kernel(parts_ref, hidden_ref, out_ref):
    total = parts_ref[0].astype(F32)
    for index in range(1, parts_ref.shape[0]):
        total = total + parts_ref[index].astype(F32)
    out_ref[...] = (hidden_ref[...].astype(F32) + total).astype(BF16)


def call(kernel, outs, inputs, scalars=0, scratch=(), limit=16, hold=True, raw=0):
    last = len(inputs) - raw
    spaces = [pltpu.SMEM] * scalars
    spaces += [pltpu.VMEM if hold else pltpu.HBM] * (last - scalars)
    spaces += [pltpu.HBM] * raw
    specs = [SMEM] * scalars + [VMEM] * (last - scalars)
    specs += [pl.BlockSpec(memory_space=pl.ANY)] * raw
    return pl.pallas_call(
        kernel,
        out_shape=tuple(pltpu.VMEM(shape, dtype) for shape, dtype in outs),
        in_specs=specs,
        out_specs=tuple(VMEM for _ in outs),
        scratch_shapes=list(scratch),
        compiler_params=pltpu.CompilerParams(vmem_limit_bytes=limit << 20),
    )(*[pltpu.with_memory_space_constraint(v, space) for v, space in zip(inputs, spaces)])


def shift(value, axis, count, step):
    return lax.ppermute(value, axis, [(i, (i + step) % count) for i in range(count)])


def local(
    queries,
    key_lift,
    value_lift,
    page_pool,
    fresh_latents,
    page_table,
    context_lengths,
    tree_parents,
    out_weight,
    residual,
    norm_gain,
    expert_ids,
    route_weights,
    gate_matrix,
    up_matrix,
    down_matrix,
):
    rows = queries.shape[0]
    row_dev, width = residual.shape
    ring, wide, deep = lax.axis_size(CONTEXT), lax.axis_size(WIDE), lax.axis_size(DEEP)
    half = rows // 2
    slots = rows // row_dev * CAP
    full = width + TAIL
    hidden_units = gate_matrix.shape[2]
    expert = lax.axis_index(EXPERT)
    places = (
        lax.axis_index(CONTEXT),
        expert,
        lax.axis_index(CORE),
        lax.axis_index(WIDE),
        2 * deep,
    )
    number = jnp.arange(8, dtype=jnp.int32)
    place = jnp.zeros((8,), jnp.int32)
    for index, value in enumerate(places):
        place = jnp.where(number == index, value, place)

    low, high = call(
        attention_kernel,
        [((VD + 16, rows), BF16)] * 2,
        [
            place,
            queries,
            key_lift,
            value_lift,
            page_pool.reshape(-1, page_pool.shape[-1]),
            fresh_latents.reshape(-1, fresh_latents.shape[-1]),
            page_table.T,
            context_lengths.reshape(1, -1),
            tree_parents.T,
        ],
        scalars=1,
        hold=False,
        limit=24,
    )

    def around(low, high):
        low1, high1 = shift(low, CONTEXT, ring, 1), shift(high, CONTEXT, ring, 1)
        low3, high3 = shift(low, CONTEXT, ring, -1), shift(high, CONTEXT, ring, -1)
        low2, high2 = shift(low1, CONTEXT, ring, 1), shift(high3, CONTEXT, ring, -1)
        return (low, low1, low2, low3), (high, high1, high2, high3)

    lows, highs = around(low, high)
    send, keep = call(
        merge_kernel,
        [((half, width), BF16), ((half, width), F32)],
        [place, *lows, *highs, out_weight],
        scalars=1,
        scratch=[
            pltpu.VMEM((wide * deep, 2, row_dev, width), F32),
            pltpu.VMEM(out_weight.shape, BF16),
            pltpu.SemaphoreType.DMA(()),
        ],
        raw=1,
    )
    cuts = call(
        cut_kernel,
        [((hidden_units, width), BF16)] * (ring - 1),
        [place, down_matrix[0], send],
        scalars=1,
    )
    others = []
    for step, cut in enumerate(cuts, 1):
        others.append(shift(cut, CONTEXT, ring, step))
    split = [((half // wide, width), F32)] + [((half // wide, width), BF16)] * (wide - 1)
    got = shift(send, CORE, 2, 1)
    own, *sends = call(add_kernel, split, [place, keep, got], scalars=1)
    received = []
    for step, part in enumerate(sends, 1):
        received.append(shift(part, WIDE, wide, step))
    chunk = [((deep, row_dev, width), BF16)]
    (summed,) = call(sum_kernel, chunk, [own, *received])
    mixed = lax.all_to_all(summed, DEEP, 0, 0, tiled=True)
    hidden, payload = call(
        hidden_kernel,
        [((row_dev, width), BF16), ((deep, row_dev, full), BF16)],
        [mixed, residual, expert_ids, route_weights],
    )
    near = lax.all_to_all(payload, DEEP, 0, 0, tiled=True).reshape(deep * row_dev, full)
    share_slots = slots // wide
    pick, *parts = call(
        select_kernel,
        [((deep * row_dev, slots), BF16)] + [((share_slots, full), BF16)] * wide,
        [place, near],
        scalars=1,
    )
    parts = [shift(part, WIDE, wide, step) if step else part for step, part in enumerate(parts)]
    low, send = call(sort_kernel, [((slots // 2, full), BF16)] * 2, parts)
    lows, highs = around(low, shift(send, CORE, 2, 1))
    active, share = call(
        expert_kernel,
        [((slots, hidden_units), BF16), ((slots, TAIL), F32)],
        [
            place,
            *[part for pair in zip(lows, highs) for part in pair],
            norm_gain.reshape(ring, 1, width),
            gate_matrix[0],
            up_matrix[0],
        ],
        scalars=1,
    )
    actives = [active] + [shift(active, CONTEXT, ring, step) for step in range(1, ring)]
    low, high = call(
        down_kernel,
        [((slots // 2, width), BF16)] * 2,
        [place, *actives, *others, down_matrix[0], share],
        scalars=1,
    )
    parts = call(
        back_kernel,
        [((share_slots, width), BF16)] * wide,
        [low, shift(high, CORE, 2, 1)],
    )
    parts = [shift(part, WIDE, wide, -step) if step else part for step, part in enumerate(parts)]
    (summed,) = call(spread_kernel, chunk, [pick, *parts])
    returned = lax.all_to_all(summed, DEEP, 0, 0, tiled=True)
    (out,) = call(output_kernel, [((row_dev, width), BF16)], [returned, hidden])
    return out


def solution(mesh):
    fine = Mesh(mesh.devices.reshape(4, 4, 8, 2), (CONTEXT, WIDE, DEEP, CORE))
    return jax.shard_map(
        local,
        mesh=fine,
        in_specs=(
            P(None, EXPERT),
            P(EXPERT, None, None),
            P(EXPERT, None, None),
            P(CONTEXT, None, None),
            P(CONTEXT, None, None),
            P(),
            P(),
            P(),
            P(EXPERT, CONTEXT),
            P(EXPERT, CONTEXT),
            P(),
            P(EXPERT, None),
            P(EXPERT, None),
            P(EXPERT, None, CONTEXT),
            P(EXPERT, None, CONTEXT),
            P(EXPERT, CONTEXT, None),
        ),
        out_specs=P(EXPERT, CONTEXT),
        check_vma=False,
    )
```

```python
import jax
import jax.numpy as jnp
from jax import lax
from jax.experimental import pallas as pl
from jax.experimental.pallas import tpu as pltpu
from jax.sharding import Mesh, PartitionSpec as P


LAT = 512
ROPE = 64
QK = 128
VD = 128
PAGE = 64
LOOK = 8
CAP = 3
NEGATIVE_FILL = -1e30
NORM_EPSILON = 1e-06
F32 = jnp.float32
BF16 = jnp.bfloat16
SMEM = pl.BlockSpec(memory_space=pltpu.SMEM)
VMEM = pl.BlockSpec(memory_space=pltpu.VMEM)
TAIL = 128


CONTEXT = "context"
WIDE = "x"
DEEP = "z"
CORE = "core"
EXPERT = (WIDE, DEEP, CORE)


def iota(shape, axis):
    return lax.broadcasted_iota(jnp.int32, shape, axis)


def dot_nn(a, b):
    return jnp.dot(a, b, preferred_element_type=F32)


def dot_nt(a, b):
    return lax.dot_general(a, b, (((1,), (1,)), ((), ())), preferred_element_type=F32)


def split3(value):
    high = value.astype(BF16)
    rest = value - high.astype(F32)
    middle = rest.astype(BF16)
    low = (rest - middle.astype(F32)).astype(BF16)
    return high, middle, low


def attention_kernel(
    place, q_ref, kl_ref, vl_ref, pool_ref, fresh_ref, table_ref, length_ref, parent_ref, *refs
):
    out_weight, *outs, held_weight, done = refs
    load = pltpu.make_async_copy(out_weight, held_weight, done)
    load.start()
    context = place[0]
    pool_rows = pool_ref.shape[0]
    fresh_rows = fresh_ref.shape[0]
    rows = q_ref.shape[0]
    table_len, leaves = table_ref.shape
    pages = pool_rows // PAGE
    passed = (iota((table_len, leaves), 0) * PAGE).astype(F32)
    remain = jnp.clip(length_ref[...].astype(F32) - passed, 0.0, float(PAGE))
    table = table_ref[...]
    line = iota((16, leaves), 0)
    limits = jnp.zeros((16, leaves), F32)
    for page in range(pages):
        seen = jnp.sum(
            jnp.where(table == context * pages + page, remain, 0.0), axis=0, keepdims=True
        )
        limits = jnp.where(line == page, seen, limits)
    spread = (iota((leaves, rows), 0) == iota((leaves, rows), 1) // LOOK).astype(F32).astype(BF16)
    row_limits = dot_nn(limits.astype(BF16), spread)
    page_limit = jnp.concatenate(
        [jnp.broadcast_to(row_limits[p : p + 1, :], (PAGE, rows)) for p in range(pages)], axis=0
    )
    within = jnp.bitwise_and(iota((pool_rows, rows), 0), PAGE - 1).astype(F32)
    page_mask = jnp.where(within < page_limit, 1.0, 0.0)
    own_leaves = fresh_rows // LOOK
    pick_leaf = (
        (iota((fresh_rows, leaves), 1) == context * own_leaves + iota((fresh_rows, leaves), 0) // LOOK)
        .astype(F32)
        .astype(BF16)
    )
    parents = dot_nt(pick_leaf, parent_ref[...].astype(F32).astype(BF16))
    token = jnp.bitwise_and(iota((fresh_rows, LOOK), 0), LOOK - 1)
    parent = jnp.sum(
        jnp.where(iota((fresh_rows, LOOK), 1) == token, parents, 0.0), axis=1, keepdims=True
    )
    square = (fresh_rows, fresh_rows)
    first = (iota(square, 0) // LOOK) * LOOK
    step = (iota(square, 1) - first).astype(F32)
    linked = jnp.where((step == parent) & (parent >= 0.0), 1.0, 0.0)
    linked = jnp.where(iota(square, 0) == iota(square, 1), 1.0, linked)
    for _ in range(3):
        half = linked.astype(BF16)
        linked = jnp.where(dot_nn(half, half) > 0.5, 1.0, 0.0)
    fresh_mask = jnp.concatenate([linked.T] * (rows // fresh_rows), axis=1)
    here = iota((fresh_rows, rows), 1) // fresh_rows == context
    fresh_mask = jnp.where(here, fresh_mask, 0.0)
    mask = jnp.concatenate([page_mask, fresh_mask], axis=0) > 0.5

    keys = jnp.concatenate([pool_ref[...], fresh_ref[...]], axis=0)
    latents = keys[:, :LAT]
    turned = keys[:, LAT:]
    scale = (QK + ROPE) ** (-0.5)
    for head, out in enumerate(outs):
        start = head * (QK + ROPE)
        plain = q_ref[:, start : start + QK]
        rotary = q_ref[:, start + QK : start + QK + ROPE]
        lifted = dot_nn(plain, kl_ref[head]).astype(BF16)
        scores = (dot_nt(latents, lifted) + dot_nt(turned, rotary)) * scale
        scores = jnp.where(mask, scores, NEGATIVE_FILL)
        best = jnp.max(scores, axis=0, keepdims=True)
        weights = jnp.exp(scores - best)
        total = jnp.sum(weights, axis=0, keepdims=True)
        values = dot_nn(latents, vl_ref[head]).T.astype(BF16)
        mixed = dot_nn(values, weights.astype(BF16)) / total
        out[:VD, :] = mixed.astype(BF16)
        high, middle, low = split3(best + jnp.log(total))
        line = iota((16, rows), 0)
        extra = jnp.where(
            line == 0,
            high.astype(F32),
            jnp.where(line == 1, middle.astype(F32), jnp.where(line == 2, low.astype(F32), 0.0)),
        )
        out[VD:, :] = extra.astype(BF16)
    load.wait()


def merge_kernel(place, *refs):
    core = place[2]
    parts, (weight_ref, send_ref, keep_ref, scratch) = refs[:8], refs[8:]
    heads = []
    for head in range(2):
        own = parts[4 * head : 4 * head + 4]
        logs = []
        for part in own:
            extra = part[VD:, :].astype(F32)
            logs.append(extra[0:1, :] + extra[1:2, :] + extra[2:3, :])
        best = jnp.maximum(jnp.maximum(logs[0], logs[1]), jnp.maximum(logs[2], logs[3]))
        shares = [jnp.exp(log - best) for log in logs]
        inverse = 1.0 / (shares[0] + shares[1] + shares[2] + shares[3])
        mixed = 0.0
        for part, share in zip(own, shares):
            mixed = mixed + part[:VD, :].astype(F32) * (share * inverse)
        heads.append(mixed)
    scratch[...] = jnp.concatenate(heads, axis=0).T.reshape(scratch.shape)
    half = send_ref.shape[0]
    sent = scratch[:, 1 - core].reshape(half, -1).astype(BF16)
    send_ref[...] = dot_nn(sent, weight_ref[...]).astype(BF16)
    kept = scratch[:, core].reshape(half, -1).astype(BF16)
    keep_ref[...] = dot_nn(kept, weight_ref[...])


def add_kernel(place, keep_ref, got_ref, own_ref, *sends):
    rows = own_ref.shape[0]
    count = len(sends) + 1
    for step in range(count):
        target = lax.rem(place[3] + step, count)
        at = pl.ds(pl.multiple_of(target * rows, rows), rows)
        total = keep_ref[at, :] + got_ref[at, :].astype(F32)
        if step == 0:
            own_ref[...] = total
        else:
            sends[step - 1][...] = total.astype(BF16)


def sum_kernel(own_ref, *refs):
    total = own_ref[...]
    for ref in refs[:-1]:
        total = total + ref[...].astype(F32)
    refs[-1][...] = total.astype(BF16).reshape(refs[-1].shape)


def cut_kernel(place, down_ref, after_ref, *outs):
    width = outs[0].shape[1]
    count = len(outs) + 1
    for step, out in enumerate(outs, 1):
        target = lax.rem(place[0] + step, count)
        out[...] = down_ref[:, pl.ds(pl.multiple_of(target * width, 128), width)]


def hidden_kernel(parts_ref, residual_ref, ids_ref, weights_ref, hidden_ref, payload_ref):
    total = residual_ref[...].astype(F32)
    mixed = parts_ref[0].astype(F32)
    for index in range(1, parts_ref.shape[0]):
        mixed = mixed + parts_ref[index].astype(F32)
    hidden = (total + mixed).astype(BF16)
    hidden_ref[...] = hidden
    floats = hidden.astype(F32)
    squares = jnp.sum(floats * floats, axis=1, keepdims=True)
    top = ids_ref.shape[1]
    row, lane = iota((top, TAIL), 0), iota((top, TAIL), 1)
    tail = dot_nn(
        ids_ref[...].astype(F32).astype(BF16), jnp.where(lane == row, 1.0, 0.0).astype(BF16)
    )
    for index, piece in enumerate(split3(weights_ref[...])):
        where = lane == row + (index + 1) * top
        tail = tail + dot_nn(piece, jnp.where(where, 1.0, 0.0).astype(BF16))
    lane = iota((hidden.shape[0], TAIL), 1)
    for index, piece in enumerate(split3(squares)):
        tail = jnp.where(lane == 4 * top + index, piece.astype(F32), tail)
    tail = tail.astype(BF16)
    width = hidden.shape[1]
    for index in range(payload_ref.shape[0]):
        payload_ref[index, :, :width] = hidden
        payload_ref[index, :, width:] = tail


def select_kernel(place, rows_ref, pick_ref, *outs):
    rows = rows_ref.shape[0]
    count = len(outs)
    slots = pick_ref.shape[1] // (2 * count)
    values = rows_ref[...]
    width = values.shape[1] - TAIL
    tails = values[:, width:].astype(F32)
    lane = iota((rows, TAIL), 1)
    base = place[1] - place[3] * place[4]
    named = jnp.zeros((rows, TAIL), F32)
    for index in range(2 * count):
        expert = lax.rem(place[3] + index // 2, count) * place[4] + base
        if index % 2:
            expert = expert + 1 - 2 * place[2]
        found = jnp.max(
            jnp.where((tails == expert.astype(F32)) & (lane < 8), 1.0, 0.0), axis=1, keepdims=True
        )
        named = jnp.where(lane == index, found, named)
    ahead = (iota((rows, rows), 1) < iota((rows, rows), 0)) & (
        iota((rows, rows), 1) // 8 == iota((rows, rows), 0) // 8
    )
    before = dot_nn(jnp.where(ahead, 1.0, 0.0).astype(BF16), named.astype(BF16))
    slot_of = before + (iota((rows, TAIL), 0) // 8 * CAP).astype(F32)
    slot = iota((rows, pick_ref.shape[1]), 1).astype(F32)
    pick = jnp.zeros((rows, pick_ref.shape[1]), F32)
    for index in range(2 * count):
        match = slot == slot_of[:, index : index + 1] + float(index * slots)
        pick = jnp.where(match & (named[:, index : index + 1] > 0.5), 1.0, pick)
    pick_ref[...] = pick.astype(BF16)
    chosen = dot_nn(pick.T.astype(BF16), values).astype(BF16)
    for step, out in enumerate(outs):
        out[...] = chosen[2 * slots * step : 2 * slots * (step + 1)]


def sort_kernel(*refs):
    parts, (low_ref, send_ref) = refs[:-2], refs[-2:]
    slots = parts[0].shape[0] // 2
    for step, part in enumerate(parts):
        low_ref[step * slots : (step + 1) * slots, :] = part[:slots, :]
        send_ref[step * slots : (step + 1) * slots, :] = part[slots:, :]


def back_kernel(low_ref, got_ref, *outs):
    slots = outs[0].shape[0] // 2
    for step, out in enumerate(outs):
        out[:slots, :] = low_ref[step * slots : (step + 1) * slots, :]
        out[slots:, :] = got_ref[step * slots : (step + 1) * slots, :]


def partial_sums(place, index, low_ref, high_ref, gain_ref, gate_ref, up_ref):
    count, width = gain_ref.shape[0], gain_ref.shape[2]
    source = lax.rem(place[0] + (count - index), count)
    rows = jnp.concatenate([low_ref[:, :width], high_ref[:, :width]], axis=0)
    scaled = (rows.astype(F32) * gain_ref[source]).astype(BF16)
    at = pl.ds(pl.multiple_of(source * width, width), width)
    return dot_nn(scaled, gate_ref[at, :]), dot_nn(scaled, up_ref[at, :])


def own_kernel(place, low_ref, high_ref, gain_ref, gate_ref, up_ref, gate_sum, up_sum):
    gate_sum[...], up_sum[...] = partial_sums(
        place, 0, low_ref, high_ref, gain_ref, gate_ref, up_ref
    )


def near_kernel(place, gate_old, up_old, low1, high1, low3, high3, *refs):
    gate_sum, up_sum = refs[3:]
    gate1, up1 = partial_sums(place, 1, low1, high1, *refs[:3])
    gate3, up3 = partial_sums(place, 3, low3, high3, *refs[:3])
    gate_sum[...] = gate_old[...] + gate1 + gate3
    up_sum[...] = up_old[...] + up1 + up3


def expert_kernel(place, gate_old, up_old, *refs):
    expert = place[1].astype(F32)
    parts = refs[:8]
    gain_ref, gate_ref, up_ref, active_ref, share_ref = refs[8:]
    slots = active_ref.shape[0]
    width = gain_ref.shape[2]
    count = 4
    lane = iota((slots, TAIL), 1)
    squares = 0.0
    for index in range(count):
        tail = jnp.concatenate([parts[2 * index][:, width:], parts[2 * index + 1][:, width:]], axis=0)
        tail = tail.astype(F32)
        squares = squares + jnp.sum(
            jnp.where((lane >= 32) & (lane < 35), tail, 0.0), axis=1, keepdims=True
        )
        if index == 0:
            shares = (
                pltpu.roll(tail, TAIL - 8, 1)
                + pltpu.roll(tail, TAIL - 16, 1)
                + pltpu.roll(tail, TAIL - 24, 1)
            )
            share = jnp.sum(
                jnp.where((tail == expert) & (lane < 8), shares, 0.0), axis=1, keepdims=True
            )
            share_ref[...] = jnp.broadcast_to(share, share_ref.shape)
    inverse = lax.rsqrt(squares * (1.0 / (count * width)) + NORM_EPSILON)
    gate2, up2 = partial_sums(place, 2, parts[4], parts[5], gain_ref, gate_ref, up_ref)
    gate_part = (gate_old[...] + gate2) * inverse
    up_part = (up_old[...] + up2) * inverse
    active_ref[...] = (gate_part / (1.0 + jnp.exp(-gate_part)) * up_part).astype(BF16)


def down_kernel(place, *refs):
    actives, others, (down_ref, share_ref, low_ref, high_ref) = refs[:4], refs[4:7], refs[7:]
    width = low_ref.shape[1]
    half = low_ref.shape[0]
    at = pl.ds(pl.multiple_of(place[0] * width, 128), width)
    made = dot_nn(actives[0][...], down_ref[:, at])
    for active, other in zip(actives[1:], others):
        made = made + dot_nn(active[...], other[...])
    made = (made * share_ref[:, :1]).astype(BF16)
    low_ref[...] = made[:half]
    high_ref[...] = made[half:]


def spread_kernel(pick_ref, *refs):
    values = jnp.concatenate([ref[...] for ref in refs[:-1]], axis=0)
    refs[-1][...] = dot_nn(pick_ref[...], values).astype(BF16).reshape(refs[-1].shape)


def output_kernel(parts_ref, hidden_ref, out_ref):
    total = parts_ref[0].astype(F32)
    for index in range(1, parts_ref.shape[0]):
        total = total + parts_ref[index].astype(F32)
    out_ref[...] = (hidden_ref[...].astype(F32) + total).astype(BF16)


def call(kernel, outs, inputs, scalars=0, scratch=(), limit=16, hold=True, raw=0, out=pltpu.VMEM):
    last = len(inputs) - raw
    spaces = [pltpu.SMEM] * scalars
    spaces += [pltpu.VMEM if hold else pltpu.HBM] * (last - scalars)
    spaces += [pltpu.HBM] * raw
    specs = [SMEM] * scalars + [VMEM] * (last - scalars)
    specs += [pl.BlockSpec(memory_space=pl.ANY)] * raw
    return pl.pallas_call(
        kernel,
        out_shape=tuple(out(shape, dtype) for shape, dtype in outs),
        in_specs=specs,
        out_specs=tuple(VMEM for _ in outs),
        scratch_shapes=list(scratch),
        compiler_params=pltpu.CompilerParams(vmem_limit_bytes=limit << 20),
    )(*[pltpu.with_memory_space_constraint(v, space) for v, space in zip(inputs, spaces)])


def shift(value, axis, count, step):
    return lax.ppermute(value, axis, [(i, (i + step) % count) for i in range(count)])


def local(
    queries,
    key_lift,
    value_lift,
    page_pool,
    fresh_latents,
    page_table,
    context_lengths,
    tree_parents,
    out_weight,
    residual,
    norm_gain,
    expert_ids,
    route_weights,
    gate_matrix,
    up_matrix,
    down_matrix,
):
    rows = queries.shape[0]
    row_dev, width = residual.shape
    ring, wide, deep = lax.axis_size(CONTEXT), lax.axis_size(WIDE), lax.axis_size(DEEP)
    half = rows // 2
    slots = rows // row_dev * CAP
    full = width + TAIL
    hidden_units = gate_matrix.shape[2]
    expert = lax.axis_index(EXPERT)
    places = (
        lax.axis_index(CONTEXT),
        expert,
        lax.axis_index(CORE),
        lax.axis_index(WIDE),
        2 * deep,
    )
    number = jnp.arange(8, dtype=jnp.int32)
    place = jnp.zeros((8,), jnp.int32)
    for index, value in enumerate(places):
        place = jnp.where(number == index, value, place)

    low, high, held_weight = call(
        attention_kernel,
        [((VD + 16, rows), BF16)] * 2 + [(out_weight.shape, BF16)],
        [
            place,
            queries,
            key_lift,
            value_lift,
            page_pool.reshape(-1, page_pool.shape[-1]),
            fresh_latents.reshape(-1, fresh_latents.shape[-1]),
            page_table.T,
            context_lengths.reshape(1, -1),
            tree_parents.T,
            out_weight,
        ],
        scalars=1,
        hold=False,
        limit=24,
        raw=1,
        scratch=[pltpu.SemaphoreType.DMA(())],
    )

    def around(low, high):
        low1, high1 = shift(low, CONTEXT, ring, 1), shift(high, CONTEXT, ring, 1)
        low3, high3 = shift(low, CONTEXT, ring, -1), shift(high, CONTEXT, ring, -1)
        low2, high2 = shift(low1, CONTEXT, ring, 1), shift(high3, CONTEXT, ring, -1)
        return (low, low1, low2, low3), (high, high1, high2, high3)

    lows, highs = around(low, high)
    send, keep = call(
        merge_kernel,
        [((half, width), BF16), ((half, width), F32)],
        [place, *lows, *highs, held_weight],
        scalars=1,
        scratch=[pltpu.VMEM((wide * deep, 2, row_dev, out_weight.shape[0]), F32)],
    )
    cuts = call(
        cut_kernel,
        [((hidden_units, width), BF16)] * (ring - 1),
        [place, down_matrix[0], send],
        scalars=1,
    )
    others = []
    for step, cut in enumerate(cuts, 1):
        others.append(shift(cut, CONTEXT, ring, step))
    split = [((half // wide, width), F32)] + [((half // wide, width), BF16)] * (wide - 1)
    got = shift(send, CORE, 2, 1)
    own, *sends = call(add_kernel, split, [place, keep, got], scalars=1)
    received = []
    for step, part in enumerate(sends, 1):
        received.append(shift(part, WIDE, wide, step))
    chunk = [((deep, row_dev, width), BF16)]
    (summed,) = call(sum_kernel, chunk, [own, *received])
    mixed = lax.all_to_all(summed, DEEP, 0, 0, tiled=True)
    hidden, payload = call(
        hidden_kernel,
        [((row_dev, width), BF16), ((deep, row_dev, full), BF16)],
        [mixed, residual, expert_ids, route_weights],
    )
    near = lax.all_to_all(payload, DEEP, 0, 0, tiled=True).reshape(deep * row_dev, full)
    share_slots = slots // wide
    pick, *parts = call(
        select_kernel,
        [((deep * row_dev, slots), BF16)] + [((share_slots, full), BF16)] * wide,
        [place, near],
        scalars=1,
    )
    parts = [shift(part, WIDE, wide, step) if step else part for step, part in enumerate(parts)]
    low, send = call(sort_kernel, [((slots // 2, full), BF16)] * 2, parts)
    lows, highs = around(low, shift(send, CORE, 2, 1))
    weights = [norm_gain.reshape(ring, 1, width), gate_matrix[0], up_matrix[0]]
    sums = [((slots, hidden_units), F32)] * 2
    partial = call(own_kernel, sums, [place, lows[0], highs[0], *weights], scalars=1)
    partial = call(
        near_kernel,
        sums,
        [place, *partial, lows[1], highs[1], lows[3], highs[3], *weights],
        scalars=1,
    )
    active, share = call(
        expert_kernel,
        [((slots, hidden_units), BF16), ((slots, TAIL), F32)],
        [place, *partial, *[part for pair in zip(lows, highs) for part in pair], *weights],
        scalars=1,
    )
    actives = [active] + [shift(active, CONTEXT, ring, step) for step in range(1, ring)]
    low, high = call(
        down_kernel,
        [((slots // 2, width), BF16)] * 2,
        [place, *actives, *others, down_matrix[0], share],
        scalars=1,
    )
    parts = call(
        back_kernel,
        [((share_slots, width), BF16)] * wide,
        [low, shift(high, CORE, 2, 1)],
    )
    parts = [shift(part, WIDE, wide, -step) if step else part for step, part in enumerate(parts)]
    (summed,) = call(spread_kernel, chunk, [pick, *parts])
    returned = lax.all_to_all(summed, DEEP, 0, 0, tiled=True)
    done = [((row_dev, width), BF16)]
    return call(output_kernel, done, [returned, hidden], out=jax.ShapeDtypeStruct)[0]


def solution(mesh):
    fine = Mesh(mesh.devices.reshape(4, 4, 8, 2), (CONTEXT, WIDE, DEEP, CORE))
    return jax.shard_map(
        local,
        mesh=fine,
        in_specs=(
            P(None, EXPERT),
            P(EXPERT, None, None),
            P(EXPERT, None, None),
            P(CONTEXT, None, None),
            P(CONTEXT, None, None),
            P(),
            P(),
            P(),
            P(EXPERT, CONTEXT),
            P(EXPERT, CONTEXT),
            P(),
            P(EXPERT, None),
            P(EXPERT, None),
            P(EXPERT, None, CONTEXT),
            P(EXPERT, None, CONTEXT),
            P(EXPERT, CONTEXT, None),
        ),
        out_specs=P(EXPERT, CONTEXT),
        check_vma=False,
    )
```

```python
import jax
import jax.numpy as jnp
from jax import lax
from jax.experimental import pallas as pl
from jax.experimental.pallas import tpu as pltpu
from jax.sharding import Mesh, PartitionSpec as P


LAT = 512
ROPE = 64
QK = 128
VD = 128
PAGE = 64
LOOK = 8
CAP = 3
NEGATIVE_FILL = -1e30
NORM_EPSILON = 1e-06
F32 = jnp.float32
BF16 = jnp.bfloat16
SMEM = pl.BlockSpec(memory_space=pltpu.SMEM)
VMEM = pl.BlockSpec(memory_space=pltpu.VMEM)
TAIL = 128


CONTEXT = "context"
WIDE = "x"
DEEP = "z"
CORE = "core"
EXPERT = (WIDE, DEEP, CORE)


def iota(shape, axis):
    return lax.broadcasted_iota(jnp.int32, shape, axis)


def dot_nn(a, b):
    return jnp.dot(a, b, preferred_element_type=F32)


def dot_nt(a, b):
    return lax.dot_general(a, b, (((1,), (1,)), ((), ())), preferred_element_type=F32)


def split3(value):
    high = value.astype(BF16)
    rest = value - high.astype(F32)
    middle = rest.astype(BF16)
    low = (rest - middle.astype(F32)).astype(BF16)
    return high, middle, low


def attention_kernel(
    place, q_ref, kl_ref, vl_ref, pool_ref, fresh_ref, table_ref, length_ref, parent_ref, *refs
):
    out_weight, out, q_next, kl_next, vl_next, keys_ref, mask_ref, held_weight, done = refs
    load = pltpu.make_async_copy(out_weight, held_weight, done)
    load.start()
    context = place[0]
    pool_rows = pool_ref.shape[0]
    fresh_rows = fresh_ref.shape[0]
    rows = q_ref.shape[0]
    table_len, leaves = table_ref.shape
    pages = pool_rows // PAGE
    passed = (iota((table_len, leaves), 0) * PAGE).astype(F32)
    remain = jnp.clip(length_ref[...].astype(F32) - passed, 0.0, float(PAGE))
    table = table_ref[...]
    line = iota((16, leaves), 0)
    limits = jnp.zeros((16, leaves), F32)
    for page in range(pages):
        seen = jnp.sum(
            jnp.where(table == context * pages + page, remain, 0.0), axis=0, keepdims=True
        )
        limits = jnp.where(line == page, seen, limits)
    spread = (iota((leaves, rows), 0) == iota((leaves, rows), 1) // LOOK).astype(F32).astype(BF16)
    row_limits = dot_nn(limits.astype(BF16), spread)
    page_limit = jnp.concatenate(
        [jnp.broadcast_to(row_limits[p : p + 1, :], (PAGE, rows)) for p in range(pages)], axis=0
    )
    within = jnp.bitwise_and(iota((pool_rows, rows), 0), PAGE - 1).astype(F32)
    page_mask = jnp.where(within < page_limit, 1.0, 0.0)
    own_leaves = fresh_rows // LOOK
    pick_leaf = (
        (iota((fresh_rows, leaves), 1) == context * own_leaves + iota((fresh_rows, leaves), 0) // LOOK)
        .astype(F32)
        .astype(BF16)
    )
    parents = dot_nt(pick_leaf, parent_ref[...].astype(F32).astype(BF16))
    token = jnp.bitwise_and(iota((fresh_rows, LOOK), 0), LOOK - 1)
    parent = jnp.sum(
        jnp.where(iota((fresh_rows, LOOK), 1) == token, parents, 0.0), axis=1, keepdims=True
    )
    square = (fresh_rows, fresh_rows)
    first = (iota(square, 0) // LOOK) * LOOK
    step = (iota(square, 1) - first).astype(F32)
    linked = jnp.where((step == parent) & (parent >= 0.0), 1.0, 0.0)
    linked = jnp.where(iota(square, 0) == iota(square, 1), 1.0, linked)
    for _ in range(3):
        half = linked.astype(BF16)
        linked = jnp.where(dot_nn(half, half) > 0.5, 1.0, 0.0)
    fresh_mask = jnp.concatenate([linked.T] * (rows // fresh_rows), axis=1)
    here = iota((fresh_rows, rows), 1) // fresh_rows == context
    fresh_mask = jnp.where(here, fresh_mask, 0.0)
    mask_ref[...] = jnp.concatenate([page_mask, fresh_mask], axis=0).astype(BF16)
    keys_ref[...] = jnp.concatenate([pool_ref[...], fresh_ref[...]], axis=0)
    second_kernel(q_ref, kl_ref.at[0], vl_ref.at[0], keys_ref, mask_ref, out)
    q_next[...] = q_ref[:, QK + ROPE :]
    kl_next[...] = kl_ref[1]
    vl_next[...] = vl_ref[1]
    load.wait()


def second_kernel(q_ref, kl_ref, vl_ref, keys_ref, mask_ref, out):
    rows = q_ref.shape[0]
    latents = keys_ref[:, :LAT]
    turned = keys_ref[:, LAT:]
    plain = q_ref[:, :QK]
    rotary = q_ref[:, QK : QK + ROPE]
    lifted = dot_nn(plain, kl_ref[...]).astype(BF16)
    scores = (dot_nt(latents, lifted) + dot_nt(turned, rotary)) * (QK + ROPE) ** (-0.5)
    scores = jnp.where(mask_ref[...].astype(F32) > 0.5, scores, NEGATIVE_FILL)
    best = jnp.max(scores, axis=0, keepdims=True)
    weights = jnp.exp(scores - best)
    total = jnp.sum(weights, axis=0, keepdims=True)
    values = dot_nn(latents, vl_ref[...]).T.astype(BF16)
    mixed = dot_nn(values, weights.astype(BF16)) / total
    out[:VD, :] = mixed.astype(BF16)
    high, middle, low = split3(best + jnp.log(total))
    line = iota((16, rows), 0)
    extra = jnp.where(
        line == 0,
        high.astype(F32),
        jnp.where(line == 1, middle.astype(F32), jnp.where(line == 2, low.astype(F32), 0.0)),
    )
    out[VD:, :] = extra.astype(BF16)


def merge_kernel(place, *refs):
    core = place[2]
    parts, (weight_ref, send_ref, rest_ref, scratch) = refs[:8], refs[8:]
    heads = []
    for head in range(2):
        own = parts[4 * head : 4 * head + 4]
        logs = []
        for part in own:
            extra = part[VD:, :].astype(F32)
            logs.append(extra[0:1, :] + extra[1:2, :] + extra[2:3, :])
        best = jnp.maximum(jnp.maximum(logs[0], logs[1]), jnp.maximum(logs[2], logs[3]))
        shares = [jnp.exp(log - best) for log in logs]
        inverse = 1.0 / (shares[0] + shares[1] + shares[2] + shares[3])
        mixed = 0.0
        for part, share in zip(own, shares):
            mixed = mixed + part[:VD, :].astype(F32) * (share * inverse)
        heads.append(mixed)
    scratch[...] = jnp.concatenate(heads, axis=0).T.reshape(scratch.shape)
    rest_ref[...] = scratch[:, core].reshape(rest_ref.shape).astype(BF16)
    sent = scratch[:, 1 - core].reshape(rest_ref.shape).astype(BF16)
    send_ref[...] = dot_nn(sent, weight_ref[...]).astype(BF16)


def keep_kernel(rest_ref, weight_ref, keep_ref):
    keep_ref[...] = dot_nn(rest_ref[...], weight_ref[...])


def add_kernel(place, keep_ref, got_ref, own_ref, *sends):
    rows = own_ref.shape[0]
    count = len(sends) + 1
    for step in range(count):
        target = lax.rem(place[3] + step, count)
        at = pl.ds(pl.multiple_of(target * rows, rows), rows)
        total = keep_ref[at, :] + got_ref[at, :].astype(F32)
        if step == 0:
            own_ref[...] = total
        else:
            sends[step - 1][...] = total.astype(BF16)


def sum_kernel(own_ref, *refs):
    total = own_ref[...]
    for ref in refs[:-1]:
        total = total + ref[...].astype(F32)
    refs[-1][...] = total.astype(BF16).reshape(refs[-1].shape)


def cut_kernel(place, down_ref, after_ref, *outs):
    width = outs[0].shape[1]
    count = len(outs) + 1
    for step, out in enumerate(outs, 1):
        target = lax.rem(place[0] + step, count)
        out[...] = down_ref[:, pl.ds(pl.multiple_of(target * width, 128), width)]


def hidden_kernel(parts_ref, residual_ref, ids_ref, weights_ref, hidden_ref, payload_ref):
    total = residual_ref[...].astype(F32)
    mixed = parts_ref[0].astype(F32)
    for index in range(1, parts_ref.shape[0]):
        mixed = mixed + parts_ref[index].astype(F32)
    hidden = (total + mixed).astype(BF16)
    hidden_ref[...] = hidden
    floats = hidden.astype(F32)
    squares = jnp.sum(floats * floats, axis=1, keepdims=True)
    top = ids_ref.shape[1]
    row, lane = iota((top, TAIL), 0), iota((top, TAIL), 1)
    tail = dot_nn(
        ids_ref[...].astype(F32).astype(BF16), jnp.where(lane == row, 1.0, 0.0).astype(BF16)
    )
    for index, piece in enumerate(split3(weights_ref[...])):
        where = lane == row + (index + 1) * top
        tail = tail + dot_nn(piece, jnp.where(where, 1.0, 0.0).astype(BF16))
    lane = iota((hidden.shape[0], TAIL), 1)
    for index, piece in enumerate(split3(squares)):
        tail = jnp.where(lane == 4 * top + index, piece.astype(F32), tail)
    tail = tail.astype(BF16)
    width = hidden.shape[1]
    for index in range(payload_ref.shape[0]):
        payload_ref[index, :, :width] = hidden
        payload_ref[index, :, width:] = tail


def select_kernel(place, rows_ref, pick_ref, *outs):
    rows = rows_ref.shape[0]
    count = len(outs)
    slots = pick_ref.shape[1] // (2 * count)
    values = rows_ref[...]
    width = values.shape[1] - TAIL
    tails = values[:, width:].astype(F32)
    lane = iota((rows, TAIL), 1)
    base = place[1] - place[3] * place[4]
    named = jnp.zeros((rows, TAIL), F32)
    for index in range(2 * count):
        expert = lax.rem(place[3] + index // 2, count) * place[4] + base
        if index % 2:
            expert = expert + 1 - 2 * place[2]
        found = jnp.max(
            jnp.where((tails == expert.astype(F32)) & (lane < 8), 1.0, 0.0), axis=1, keepdims=True
        )
        named = jnp.where(lane == index, found, named)
    ahead = (iota((rows, rows), 1) < iota((rows, rows), 0)) & (
        iota((rows, rows), 1) // 8 == iota((rows, rows), 0) // 8
    )
    before = dot_nn(jnp.where(ahead, 1.0, 0.0).astype(BF16), named.astype(BF16))
    slot_of = before + (iota((rows, TAIL), 0) // 8 * CAP).astype(F32)
    slot = iota((rows, pick_ref.shape[1]), 1).astype(F32)
    pick = jnp.zeros((rows, pick_ref.shape[1]), F32)
    for index in range(2 * count):
        match = slot == slot_of[:, index : index + 1] + float(index * slots)
        pick = jnp.where(match & (named[:, index : index + 1] > 0.5), 1.0, pick)
    pick_ref[...] = pick.astype(BF16)
    chosen = dot_nn(pick.T.astype(BF16), values).astype(BF16)
    for step, out in enumerate(outs):
        out[...] = chosen[2 * slots * step : 2 * slots * (step + 1)]


def sort_kernel(*refs):
    parts, (low_ref, send_ref) = refs[:-2], refs[-2:]
    slots = parts[0].shape[0] // 2
    for step, part in enumerate(parts):
        low_ref[step * slots : (step + 1) * slots, :] = part[:slots, :]
        send_ref[step * slots : (step + 1) * slots, :] = part[slots:, :]


def back_kernel(low_ref, got_ref, *outs):
    slots = outs[0].shape[0] // 2
    for step, out in enumerate(outs):
        out[:slots, :] = low_ref[step * slots : (step + 1) * slots, :]
        out[slots:, :] = got_ref[step * slots : (step + 1) * slots, :]


def partial_sums(place, index, low_ref, high_ref, gain_ref, gate_ref, up_ref):
    count, width = gain_ref.shape[0], gain_ref.shape[2]
    source = lax.rem(place[0] + (count - index), count)
    rows = jnp.concatenate([low_ref[:, :width], high_ref[:, :width]], axis=0)
    scaled = (rows.astype(F32) * gain_ref[source]).astype(BF16)
    at = pl.ds(pl.multiple_of(source * width, width), width)
    return dot_nn(scaled, gate_ref[at, :]), dot_nn(scaled, up_ref[at, :])


def own_kernel(place, low_ref, high_ref, gain_ref, gate_ref, up_ref, gate_sum, up_sum):
    gate_sum[...], up_sum[...] = partial_sums(
        place, 0, low_ref, high_ref, gain_ref, gate_ref, up_ref
    )


def squares_of(low_ref, high_ref, width):
    tail = jnp.concatenate([low_ref[:, width:], high_ref[:, width:]], axis=0).astype(F32)
    lane = iota(tail.shape, 1)
    return tail, jnp.sum(jnp.where((lane >= 32) & (lane < 35), tail, 0.0), axis=1, keepdims=True)


def near_kernel(place, gate_old, up_old, low0, high0, low1, high1, low3, high3, *refs):
    gate_sum, up_sum, squares_ref, share_ref = refs[3:]
    gate1, up1 = partial_sums(place, 1, low1, high1, *refs[:3])
    gate3, up3 = partial_sums(place, 3, low3, high3, *refs[:3])
    gate_sum[...] = gate_old[...] + gate1 + gate3
    up_sum[...] = up_old[...] + up1 + up3
    width = refs[0].shape[2]
    tail, squares = squares_of(low0, high0, width)
    squares = squares + squares_of(low1, high1, width)[1] + squares_of(low3, high3, width)[1]
    squares_ref[...] = jnp.broadcast_to(squares, squares_ref.shape)
    shares = (
        pltpu.roll(tail, TAIL - 8, 1)
        + pltpu.roll(tail, TAIL - 16, 1)
        + pltpu.roll(tail, TAIL - 24, 1)
    )
    named = (tail == place[1].astype(F32)) & (iota(tail.shape, 1) < 8)
    share = jnp.sum(jnp.where(named, shares, 0.0), axis=1, keepdims=True)
    share_ref[...] = jnp.broadcast_to(share, share_ref.shape)


def expert_kernel(place, gate_old, up_old, squares_ref, low2, high2, *refs):
    gain_ref, active_ref = refs[0], refs[3]
    count, width = gain_ref.shape[0], gain_ref.shape[2]
    squares = squares_ref[:, :1] + squares_of(low2, high2, width)[1]
    inverse = lax.rsqrt(squares * (1.0 / (count * width)) + NORM_EPSILON)
    gate2, up2 = partial_sums(place, 2, low2, high2, *refs[:3])
    gate_part = (gate_old[...] + gate2) * inverse
    up_part = (up_old[...] + up2) * inverse
    active_ref[...] = (gate_part / (1.0 + jnp.exp(-gate_part)) * up_part).astype(BF16)


def first_kernel(place, active0, active1, active3, other1, other3, down_ref, sum_ref):
    width = sum_ref.shape[1]
    at = pl.ds(pl.multiple_of(place[0] * width, 128), width)
    made = dot_nn(active0[...], down_ref[:, at])
    made = made + dot_nn(active1[...], other1[...])
    sum_ref[...] = made + dot_nn(active3[...], other3[...])


def down_kernel(sum_ref, active2, other2, share_ref, low_ref, high_ref):
    made = sum_ref[...] + dot_nn(active2[...], other2[...])
    made = (made * share_ref[:, :1]).astype(BF16)
    half = low_ref.shape[0]
    low_ref[...] = made[:half]
    high_ref[...] = made[half:]


def spread_kernel(pick_ref, *refs):
    values = jnp.concatenate([ref[...] for ref in refs[:-1]], axis=0)
    refs[-1][...] = dot_nn(pick_ref[...], values).astype(BF16).reshape(refs[-1].shape)


def output_kernel(parts_ref, hidden_ref, out_ref):
    total = parts_ref[0].astype(F32)
    for index in range(1, parts_ref.shape[0]):
        total = total + parts_ref[index].astype(F32)
    out_ref[...] = (hidden_ref[...].astype(F32) + total).astype(BF16)


def call(kernel, outs, inputs, scalars=0, scratch=(), limit=16, hold=True, raw=0, out=pltpu.VMEM):
    last = len(inputs) - raw
    spaces = [pltpu.SMEM] * scalars
    spaces += [pltpu.VMEM if hold else pltpu.HBM] * (last - scalars)
    spaces += [pltpu.HBM] * raw
    specs = [SMEM] * scalars + [VMEM] * (last - scalars)
    specs += [pl.BlockSpec(memory_space=pl.ANY)] * raw
    return pl.pallas_call(
        kernel,
        out_shape=tuple(out(shape, dtype) for shape, dtype in outs),
        in_specs=specs,
        out_specs=tuple(VMEM for _ in outs),
        scratch_shapes=list(scratch),
        compiler_params=pltpu.CompilerParams(vmem_limit_bytes=limit << 20),
    )(*[pltpu.with_memory_space_constraint(v, space) for v, space in zip(inputs, spaces)])


def shift(value, axis, count, step):
    return lax.ppermute(value, axis, [(i, (i + step) % count) for i in range(count)])


def local(
    queries,
    key_lift,
    value_lift,
    page_pool,
    fresh_latents,
    page_table,
    context_lengths,
    tree_parents,
    out_weight,
    residual,
    norm_gain,
    expert_ids,
    route_weights,
    gate_matrix,
    up_matrix,
    down_matrix,
):
    rows = queries.shape[0]
    row_dev, width = residual.shape
    ring, wide, deep = lax.axis_size(CONTEXT), lax.axis_size(WIDE), lax.axis_size(DEEP)
    half = rows // 2
    slots = rows // row_dev * CAP
    full = width + TAIL
    hidden_units = gate_matrix.shape[2]
    expert = lax.axis_index(EXPERT)
    places = (
        lax.axis_index(CONTEXT),
        expert,
        lax.axis_index(CORE),
        lax.axis_index(WIDE),
        2 * deep,
    )
    number = jnp.arange(8, dtype=jnp.int32)
    place = jnp.zeros((8,), jnp.int32)
    for index, value in enumerate(places):
        place = jnp.where(number == index, value, place)

    pool = page_pool.reshape(-1, page_pool.shape[-1])
    fresh = fresh_latents.reshape(-1, fresh_latents.shape[-1])
    key_rows = pool.shape[0] + fresh.shape[0]
    piece = ((VD + 16, rows), BF16)
    low, *rest, held_weight = call(
        attention_kernel,
        [
            piece,
            ((rows, QK + ROPE), BF16),
            (key_lift.shape[1:], BF16),
            (value_lift.shape[1:], BF16),
            ((key_rows, pool.shape[1]), BF16),
            ((key_rows, rows), BF16),
            (out_weight.shape, BF16),
        ],
        [
            place,
            queries,
            key_lift,
            value_lift,
            pool,
            fresh,
            page_table.T,
            context_lengths.reshape(1, -1),
            tree_parents.T,
            out_weight,
        ],
        scalars=1,
        hold=False,
        limit=24,
        raw=1,
        scratch=[pltpu.SemaphoreType.DMA(())],
    )
    (high,) = call(second_kernel, [piece], rest)

    def around(low, high):
        low1 = shift(low, CONTEXT, ring, 1)
        low3 = shift(low, CONTEXT, ring, -1)
        high1, high3 = shift(high, CONTEXT, ring, 1), shift(high, CONTEXT, ring, -1)
        low2 = shift(low1, CONTEXT, ring, 1)
        high2 = shift(high3, CONTEXT, ring, -1)
        return (low, low1, low2, low3), (high, high1, high2, high3)

    lows, highs = around(low, high)
    send, rest = call(
        merge_kernel,
        [((half, width), BF16), ((half, out_weight.shape[0]), BF16)],
        [place, *lows, *highs, held_weight],
        scalars=1,
        scratch=[pltpu.VMEM((wide * deep, 2, row_dev, out_weight.shape[0]), F32)],
    )
    cuts = call(
        cut_kernel,
        [((hidden_units, width), BF16)] * (ring - 1),
        [place, down_matrix[0], send],
        scalars=1,
    )
    others = []
    for step, cut in enumerate(cuts, 1):
        others.append(shift(cut, CONTEXT, ring, step))
    split = [((half // wide, width), F32)] + [((half // wide, width), BF16)] * (wide - 1)
    got = shift(send, CORE, 2, 1)
    (keep,) = call(keep_kernel, [((half, width), F32)], [rest, held_weight])
    own, *sends = call(add_kernel, split, [place, keep, got], scalars=1)
    received = []
    for step, part in enumerate(sends, 1):
        received.append(shift(part, WIDE, wide, step))
    chunk = [((deep, row_dev, width), BF16)]
    (summed,) = call(sum_kernel, chunk, [own, *received])
    mixed = lax.all_to_all(summed, DEEP, 0, 0, tiled=True)
    hidden, payload = call(
        hidden_kernel,
        [((row_dev, width), BF16), ((deep, row_dev, full), BF16)],
        [mixed, residual, expert_ids, route_weights],
    )
    near = lax.all_to_all(payload, DEEP, 0, 0, tiled=True).reshape(deep * row_dev, full)
    share_slots = slots // wide
    pick, *parts = call(
        select_kernel,
        [((deep * row_dev, slots), BF16)] + [((share_slots, full), BF16)] * wide,
        [place, near],
        scalars=1,
    )
    parts = [shift(part, WIDE, wide, step) if step else part for step, part in enumerate(parts)]
    low, send = call(sort_kernel, [((slots // 2, full), BF16)] * 2, parts)
    lows, highs = around(low, shift(send, CORE, 2, 1))
    weights = [norm_gain.reshape(ring, 1, width), gate_matrix[0], up_matrix[0]]
    sums = [((slots, hidden_units), F32)] * 2
    partial = call(own_kernel, sums, [place, lows[0], highs[0], *weights], scalars=1)
    *partial, squares, share = call(
        near_kernel,
        sums + [((slots, TAIL), F32)] * 2,
        [place, *partial]
        + [lows[0], highs[0], lows[1], highs[1], lows[3], highs[3]]
        + weights,
        scalars=1,
    )
    (active,) = call(
        expert_kernel,
        [((slots, hidden_units), BF16)],
        [place, *partial, squares, lows[2], highs[2], *weights],
        scalars=1,
    )
    active2 = shift(active, CONTEXT, ring, 2)
    active1, active3 = (shift(active, CONTEXT, ring, step) for step in (1, 3))
    (made,) = call(
        first_kernel,
        [((slots, width), F32)],
        [place, active, active1, active3, others[0], others[2], down_matrix[0]],
        scalars=1,
    )
    low, high = call(
        down_kernel,
        [((slots // 2, width), BF16)] * 2,
        [made, active2, others[1], share],
    )
    parts = call(
        back_kernel,
        [((share_slots, width), BF16)] * wide,
        [low, shift(high, CORE, 2, 1)],
    )
    parts = [shift(part, WIDE, wide, -step) if step else part for step, part in enumerate(parts)]
    (summed,) = call(spread_kernel, chunk, [pick, *parts])
    returned = lax.all_to_all(summed, DEEP, 0, 0, tiled=True)
    done = [((row_dev, width), BF16)]
    return call(output_kernel, done, [returned, hidden], out=jax.ShapeDtypeStruct)[0]


def solution(mesh):
    fine = Mesh(mesh.devices.reshape(4, 4, 8, 2), (CONTEXT, WIDE, DEEP, CORE))
    return jax.shard_map(
        local,
        mesh=fine,
        in_specs=(
            P(None, EXPERT),
            P(EXPERT, None, None),
            P(EXPERT, None, None),
            P(CONTEXT, None, None),
            P(CONTEXT, None, None),
            P(),
            P(),
            P(),
            P(EXPERT, CONTEXT),
            P(EXPERT, CONTEXT),
            P(),
            P(EXPERT, None),
            P(EXPERT, None),
            P(EXPERT, None, CONTEXT),
            P(EXPERT, None, CONTEXT),
            P(EXPERT, CONTEXT, None),
        ),
        out_specs=P(EXPERT, CONTEXT),
        check_vma=False,
    )
```

```python
import jax
import jax.numpy as jnp
from jax import lax
from jax.experimental import pallas as pl
from jax.experimental.pallas import tpu as pltpu
from jax.sharding import Mesh, PartitionSpec as P


LAT = 512
ROPE = 64
QK = 128
VD = 128
PAGE = 64
LOOK = 8
CAP = 3
NEGATIVE_FILL = -1e30
NORM_EPSILON = 1e-06
F32 = jnp.float32
BF16 = jnp.bfloat16
SMEM = pl.BlockSpec(memory_space=pltpu.SMEM)
VMEM = pl.BlockSpec(memory_space=pltpu.VMEM)
TAIL = 128


CONTEXT = "context"
WIDE = "x"
DEEP = "z"
CORE = "core"
EXPERT = (WIDE, DEEP, CORE)


def iota(shape, axis):
    return lax.broadcasted_iota(jnp.int32, shape, axis)


def dot_nn(a, b):
    return jnp.dot(a, b, preferred_element_type=F32)


def dot_nt(a, b):
    return lax.dot_general(a, b, (((1,), (1,)), ((), ())), preferred_element_type=F32)


def split3(value):
    high = value.astype(BF16)
    rest = value - high.astype(F32)
    middle = rest.astype(BF16)
    low = (rest - middle.astype(F32)).astype(BF16)
    return high, middle, low


def attention_kernel(
    place, q_ref, kl_ref, vl_ref, pool_ref, fresh_ref, table_ref, length_ref, parent_ref, *refs
):
    out_weight, *outs, held_weight, keys_ref, mask_ref, done = refs
    load = pltpu.make_async_copy(out_weight, held_weight, done)
    load.start()
    context = place[0]
    pool_rows = pool_ref.shape[0]
    fresh_rows = fresh_ref.shape[0]
    rows = q_ref.shape[0]
    table_len, leaves = table_ref.shape
    pages = pool_rows // PAGE
    passed = (iota((table_len, leaves), 0) * PAGE).astype(F32)
    remain = jnp.clip(length_ref[...].astype(F32) - passed, 0.0, float(PAGE))
    table = table_ref[...]
    line = iota((16, leaves), 0)
    limits = jnp.zeros((16, leaves), F32)
    for page in range(pages):
        seen = jnp.sum(
            jnp.where(table == context * pages + page, remain, 0.0), axis=0, keepdims=True
        )
        limits = jnp.where(line == page, seen, limits)
    spread = (iota((leaves, rows), 0) == iota((leaves, rows), 1) // LOOK).astype(F32).astype(BF16)
    row_limits = dot_nn(limits.astype(BF16), spread)
    page_limit = jnp.concatenate(
        [jnp.broadcast_to(row_limits[p : p + 1, :], (PAGE, rows)) for p in range(pages)], axis=0
    )
    within = jnp.bitwise_and(iota((pool_rows, rows), 0), PAGE - 1).astype(F32)
    page_mask = jnp.where(within < page_limit, 1.0, 0.0)
    own_leaves = fresh_rows // LOOK
    pick_leaf = (
        (iota((fresh_rows, leaves), 1) == context * own_leaves + iota((fresh_rows, leaves), 0) // LOOK)
        .astype(F32)
        .astype(BF16)
    )
    parents = dot_nt(pick_leaf, parent_ref[...].astype(F32).astype(BF16))
    token = jnp.bitwise_and(iota((fresh_rows, LOOK), 0), LOOK - 1)
    parent = jnp.sum(
        jnp.where(iota((fresh_rows, LOOK), 1) == token, parents, 0.0), axis=1, keepdims=True
    )
    square = (fresh_rows, fresh_rows)
    first = (iota(square, 0) // LOOK) * LOOK
    step = (iota(square, 1) - first).astype(F32)
    linked = jnp.where((step == parent) & (parent >= 0.0), 1.0, 0.0)
    linked = jnp.where(iota(square, 0) == iota(square, 1), 1.0, linked)
    for _ in range(3):
        half = linked.astype(BF16)
        linked = jnp.where(dot_nn(half, half) > 0.5, 1.0, 0.0)
    fresh_mask = jnp.concatenate([linked.T] * (rows // fresh_rows), axis=1)
    here = iota((fresh_rows, rows), 1) // fresh_rows == context
    fresh_mask = jnp.where(here, fresh_mask, 0.0)
    mask_ref[...] = jnp.concatenate([page_mask, fresh_mask], axis=0).astype(BF16)
    keys_ref[...] = jnp.concatenate([pool_ref[...], fresh_ref[...]], axis=0)
    for head, out in enumerate(outs):
        attend(head, q_ref, kl_ref, vl_ref, keys_ref, mask_ref, out)
    load.wait()


def attend(head, q_ref, kl_ref, vl_ref, keys_ref, mask_ref, out):
    rows = q_ref.shape[0]
    latents = keys_ref[:, :LAT]
    turned = keys_ref[:, LAT:]
    start = head * (QK + ROPE)
    plain = q_ref[:, start : start + QK]
    rotary = q_ref[:, start + QK : start + QK + ROPE]
    lifted = dot_nn(plain, kl_ref[head]).astype(BF16)
    scores = (dot_nt(latents, lifted) + dot_nt(turned, rotary)) * (QK + ROPE) ** (-0.5)
    scores = jnp.where(mask_ref[...].astype(F32) > 0.5, scores, NEGATIVE_FILL)
    best = jnp.max(scores, axis=0, keepdims=True)
    weights = jnp.exp(scores - best)
    total = jnp.sum(weights, axis=0, keepdims=True)
    values = dot_nn(latents, vl_ref[head]).T.astype(BF16)
    mixed = dot_nn(values, weights.astype(BF16)) / total
    out[:VD, :] = mixed.astype(BF16)
    high, middle, low = split3(best + jnp.log(total))
    line = iota((16, rows), 0)
    extra = jnp.where(
        line == 0,
        high.astype(F32),
        jnp.where(line == 1, middle.astype(F32), jnp.where(line == 2, low.astype(F32), 0.0)),
    )
    out[VD:, :] = extra.astype(BF16)


def merge_kernel(place, *refs):
    core = place[2]
    parts, (weight_ref, send_ref, rest_ref, scratch) = refs[:8], refs[8:]
    heads = []
    for head in range(2):
        own = parts[4 * head : 4 * head + 4]
        logs = []
        for part in own:
            extra = part[VD:, :].astype(F32)
            logs.append(extra[0:1, :] + extra[1:2, :] + extra[2:3, :])
        best = jnp.maximum(jnp.maximum(logs[0], logs[1]), jnp.maximum(logs[2], logs[3]))
        shares = [jnp.exp(log - best) for log in logs]
        inverse = 1.0 / (shares[0] + shares[1] + shares[2] + shares[3])
        mixed = 0.0
        for part, share in zip(own, shares):
            mixed = mixed + part[:VD, :].astype(F32) * (share * inverse)
        heads.append(mixed)
    scratch[...] = jnp.concatenate(heads, axis=0).T.reshape(scratch.shape)
    rest_ref[...] = scratch[:, core].reshape(rest_ref.shape).astype(BF16)
    sent = scratch[:, 1 - core].reshape(rest_ref.shape).astype(BF16)
    send_ref[...] = dot_nn(sent, weight_ref[...]).astype(BF16)


def keep_kernel(rest_ref, weight_ref, keep_ref):
    keep_ref[...] = dot_nn(rest_ref[...], weight_ref[...])


def add_kernel(place, keep_ref, got_ref, own_ref, *sends):
    rows = own_ref.shape[0]
    count = len(sends) + 1
    for step in range(count):
        target = lax.rem(place[3] + step, count)
        at = pl.ds(pl.multiple_of(target * rows, rows), rows)
        total = keep_ref[at, :] + got_ref[at, :].astype(F32)
        if step == 0:
            own_ref[...] = total
        else:
            sends[step - 1][...] = total.astype(BF16)


def sum_kernel(own_ref, *refs):
    total = own_ref[...]
    for ref in refs[:-1]:
        total = total + ref[...].astype(F32)
    refs[-1][...] = total.astype(BF16).reshape(refs[-1].shape)


def cut_kernel(place, down_ref, after_ref, *outs):
    width = outs[0].shape[1]
    count = len(outs) + 1
    for step, out in enumerate(outs, 1):
        target = lax.rem(place[0] + step, count)
        out[...] = down_ref[:, pl.ds(pl.multiple_of(target * width, 128), width)]


def hidden_kernel(parts_ref, residual_ref, ids_ref, weights_ref, hidden_ref, payload_ref):
    total = residual_ref[...].astype(F32)
    mixed = parts_ref[0].astype(F32)
    for index in range(1, parts_ref.shape[0]):
        mixed = mixed + parts_ref[index].astype(F32)
    hidden = (total + mixed).astype(BF16)
    hidden_ref[...] = hidden
    floats = hidden.astype(F32)
    squares = jnp.sum(floats * floats, axis=1, keepdims=True)
    top = ids_ref.shape[1]
    row, lane = iota((top, TAIL), 0), iota((top, TAIL), 1)
    tail = dot_nn(
        ids_ref[...].astype(F32).astype(BF16), jnp.where(lane == row, 1.0, 0.0).astype(BF16)
    )
    for index, piece in enumerate(split3(weights_ref[...])):
        where = lane == row + (index + 1) * top
        tail = tail + dot_nn(piece, jnp.where(where, 1.0, 0.0).astype(BF16))
    lane = iota((hidden.shape[0], TAIL), 1)
    for index, piece in enumerate(split3(squares)):
        tail = jnp.where(lane == 4 * top + index, piece.astype(F32), tail)
    tail = tail.astype(BF16)
    width = hidden.shape[1]
    for index in range(payload_ref.shape[0]):
        payload_ref[index, :, :width] = hidden
        payload_ref[index, :, width:] = tail


def select_kernel(place, rows_ref, pick_ref, *outs):
    rows = rows_ref.shape[0]
    count = len(outs)
    slots = pick_ref.shape[1] // (2 * count)
    values = rows_ref[...]
    width = values.shape[1] - TAIL
    tails = values[:, width:].astype(F32)
    lane = iota((rows, TAIL), 1)
    base = place[1] - place[3] * place[4]
    named = jnp.zeros((rows, TAIL), F32)
    for index in range(2 * count):
        expert = lax.rem(place[3] + index // 2, count) * place[4] + base
        if index % 2:
            expert = expert + 1 - 2 * place[2]
        found = jnp.max(
            jnp.where((tails == expert.astype(F32)) & (lane < 8), 1.0, 0.0), axis=1, keepdims=True
        )
        named = jnp.where(lane == index, found, named)
    ahead = (iota((rows, rows), 1) < iota((rows, rows), 0)) & (
        iota((rows, rows), 1) // 8 == iota((rows, rows), 0) // 8
    )
    before = dot_nn(jnp.where(ahead, 1.0, 0.0).astype(BF16), named.astype(BF16))
    slot_of = before + (iota((rows, TAIL), 0) // 8 * CAP).astype(F32)
    slot = iota((rows, pick_ref.shape[1]), 1).astype(F32)
    pick = jnp.zeros((rows, pick_ref.shape[1]), F32)
    for index in range(2 * count):
        match = slot == slot_of[:, index : index + 1] + float(index * slots)
        pick = jnp.where(match & (named[:, index : index + 1] > 0.5), 1.0, pick)
    pick_ref[...] = pick.astype(BF16)
    chosen = dot_nn(pick.T.astype(BF16), values).astype(BF16)
    for step, out in enumerate(outs):
        out[...] = chosen[2 * slots * step : 2 * slots * (step + 1)]


def sort_kernel(*refs):
    parts, (low_ref, send_ref) = refs[:-2], refs[-2:]
    slots = parts[0].shape[0] // 2
    for step, part in enumerate(parts):
        low_ref[step * slots : (step + 1) * slots, :] = part[:slots, :]
        send_ref[step * slots : (step + 1) * slots, :] = part[slots:, :]


def back_kernel(low_ref, got_ref, *outs):
    slots = outs[0].shape[0] // 2
    for step, out in enumerate(outs):
        out[:slots, :] = low_ref[step * slots : (step + 1) * slots, :]
        out[slots:, :] = got_ref[step * slots : (step + 1) * slots, :]


def partial_sums(place, index, low_ref, high_ref, gain_ref, gate_ref, up_ref):
    count, width = gain_ref.shape[0], gain_ref.shape[2]
    source = lax.rem(place[0] + count + index * (2 * place[2] - 1), count)
    rows = jnp.concatenate([low_ref[:, :width], high_ref[:, :width]], axis=0)
    scaled = (rows.astype(F32) * gain_ref[source]).astype(BF16)
    at = pl.ds(pl.multiple_of(source * width, width), width)
    return dot_nn(scaled, gate_ref[at, :]), dot_nn(scaled, up_ref[at, :])


def own_kernel(place, low_ref, high_ref, gain_ref, gate_ref, up_ref, gate_sum, up_sum):
    gate_sum[...], up_sum[...] = partial_sums(
        place, 0, low_ref, high_ref, gain_ref, gate_ref, up_ref
    )


def squares_of(low_ref, high_ref, width):
    tail = jnp.concatenate([low_ref[:, width:], high_ref[:, width:]], axis=0).astype(F32)
    lane = iota(tail.shape, 1)
    return tail, jnp.sum(jnp.where((lane >= 32) & (lane < 35), tail, 0.0), axis=1, keepdims=True)


def near_kernel(place, gate_old, up_old, low0, high0, low1, high1, low3, high3, *refs):
    gate_sum, up_sum, squares_ref, share_ref = refs[3:]
    gate1, up1 = partial_sums(place, 1, low1, high1, *refs[:3])
    gate3, up3 = partial_sums(place, 3, low3, high3, *refs[:3])
    gate_sum[...] = gate_old[...] + gate1 + gate3
    up_sum[...] = up_old[...] + up1 + up3
    width = refs[0].shape[2]
    tail, squares = squares_of(low0, high0, width)
    squares = squares + squares_of(low1, high1, width)[1] + squares_of(low3, high3, width)[1]
    squares_ref[...] = jnp.broadcast_to(squares, squares_ref.shape)
    shares = (
        pltpu.roll(tail, TAIL - 8, 1)
        + pltpu.roll(tail, TAIL - 16, 1)
        + pltpu.roll(tail, TAIL - 24, 1)
    )
    named = (tail == place[1].astype(F32)) & (iota(tail.shape, 1) < 8)
    share = jnp.sum(jnp.where(named, shares, 0.0), axis=1, keepdims=True)
    share_ref[...] = jnp.broadcast_to(share, share_ref.shape)


def expert_kernel(place, gate_old, up_old, squares_ref, low2, high2, *refs):
    gain_ref, active_ref = refs[0], refs[3]
    count, width = gain_ref.shape[0], gain_ref.shape[2]
    squares = squares_ref[:, :1] + squares_of(low2, high2, width)[1]
    inverse = lax.rsqrt(squares * (1.0 / (count * width)) + NORM_EPSILON)
    gate2, up2 = partial_sums(place, 2, low2, high2, *refs[:3])
    gate_part = (gate_old[...] + gate2) * inverse
    up_part = (up_old[...] + up2) * inverse
    active_ref[...] = (gate_part / (1.0 + jnp.exp(-gate_part)) * up_part).astype(BF16)


def first_kernel(place, active0, active1, active3, other1, other3, down_ref, sum_ref):
    width = sum_ref.shape[1]
    at = pl.ds(pl.multiple_of(place[0] * width, 128), width)
    made = dot_nn(active0[...], down_ref[:, at])
    made = made + dot_nn(active1[...], other1[...])
    sum_ref[...] = made + dot_nn(active3[...], other3[...])


def down_kernel(sum_ref, active2, other2, share_ref, low_ref, high_ref):
    made = sum_ref[...] + dot_nn(active2[...], other2[...])
    made = (made * share_ref[:, :1]).astype(BF16)
    half = low_ref.shape[0]
    low_ref[...] = made[:half]
    high_ref[...] = made[half:]


def spread_kernel(pick_ref, *refs):
    values = jnp.concatenate([ref[...] for ref in refs[:-1]], axis=0)
    refs[-1][...] = dot_nn(pick_ref[...], values).astype(BF16).reshape(refs[-1].shape)


def output_kernel(parts_ref, hidden_ref, out_ref):
    total = parts_ref[0].astype(F32)
    for index in range(1, parts_ref.shape[0]):
        total = total + parts_ref[index].astype(F32)
    out_ref[...] = (hidden_ref[...].astype(F32) + total).astype(BF16)


def call(kernel, outs, inputs, scalars=0, scratch=(), limit=16, hold=True, raw=0, out=pltpu.VMEM):
    last = len(inputs) - raw
    spaces = [pltpu.SMEM] * scalars
    spaces += [pltpu.VMEM if hold else pltpu.HBM] * (last - scalars)
    spaces += [pltpu.HBM] * raw
    specs = [SMEM] * scalars + [VMEM] * (last - scalars)
    specs += [pl.BlockSpec(memory_space=pl.ANY)] * raw
    return pl.pallas_call(
        kernel,
        out_shape=tuple(out(shape, dtype) for shape, dtype in outs),
        in_specs=specs,
        out_specs=tuple(VMEM for _ in outs),
        scratch_shapes=list(scratch),
        compiler_params=pltpu.CompilerParams(vmem_limit_bytes=limit << 20),
    )(*[pltpu.with_memory_space_constraint(v, space) for v, space in zip(inputs, spaces)])


def shift(value, axis, count, step):
    return lax.ppermute(value, axis, [(i, (i + step) % count) for i in range(count)])


def local(
    queries,
    key_lift,
    value_lift,
    page_pool,
    fresh_latents,
    page_table,
    context_lengths,
    tree_parents,
    out_weight,
    residual,
    norm_gain,
    expert_ids,
    route_weights,
    gate_matrix,
    up_matrix,
    down_matrix,
):
    rows = queries.shape[0]
    row_dev, width = residual.shape
    ring, wide, deep = lax.axis_size(CONTEXT), lax.axis_size(WIDE), lax.axis_size(DEEP)
    half = rows // 2
    slots = rows // row_dev * CAP
    full = width + TAIL
    hidden_units = gate_matrix.shape[2]
    expert = lax.axis_index(EXPERT)
    places = (
        lax.axis_index(CONTEXT),
        expert,
        lax.axis_index(CORE),
        lax.axis_index(WIDE),
        2 * deep,
    )
    number = jnp.arange(8, dtype=jnp.int32)
    place = jnp.zeros((8,), jnp.int32)
    for index, value in enumerate(places):
        place = jnp.where(number == index, value, place)

    pool = page_pool.reshape(-1, page_pool.shape[-1])
    fresh = fresh_latents.reshape(-1, fresh_latents.shape[-1])
    key_rows = pool.shape[0] + fresh.shape[0]
    low, high, held_weight = call(
        attention_kernel,
        [((VD + 16, rows), BF16)] * 2 + [(out_weight.shape, BF16)],
        [
            place,
            queries,
            key_lift,
            value_lift,
            pool,
            fresh,
            page_table.T,
            context_lengths.reshape(1, -1),
            tree_parents.T,
            out_weight,
        ],
        scalars=1,
        hold=False,
        limit=24,
        raw=1,
        scratch=[
            pltpu.VMEM((key_rows, pool.shape[1]), BF16),
            pltpu.VMEM((key_rows, rows), BF16),
            pltpu.SemaphoreType.DMA(()),
        ],
    )

    def around(low, high, turn):
        low1, high3 = turn(low, 1), turn(high, -1)
        high1, low3 = turn(high, 1), turn(low, -1)
        low2, high2 = turn(low1, 1), turn(high3, -1)
        return (low, low1, low2, low3), (high, high1, high2, high3)

    def across(parts, sign):
        moved = []
        for step, part in enumerate(parts, 1):
            moved.append(shift(part, WIDE, wide, sign * step))
        return moved

    def same(value, step):
        return shift(value, CONTEXT, ring, step)

    def mirrored(value, step):
        pairs = [
            (2 * at + side, 2 * ((at + step * (1 - 2 * side)) % ring) + side)
            for at in range(ring)
            for side in range(2)
        ]
        return lax.ppermute(value, (CONTEXT, CORE), pairs)

    lows, highs = around(low, high, same)
    send, rest = call(
        merge_kernel,
        [((half, width), BF16), ((half, out_weight.shape[0]), BF16)],
        [place, *lows, *highs, held_weight],
        scalars=1,
        scratch=[pltpu.VMEM((wide * deep, 2, row_dev, out_weight.shape[0]), F32)],
    )
    cuts = call(
        cut_kernel,
        [((hidden_units, width), BF16)] * (ring - 1),
        [place, down_matrix[0], send],
        scalars=1,
    )
    others = []
    for step, cut in enumerate(cuts, 1):
        others.append(shift(cut, CONTEXT, ring, step))
    split = [((half // wide, width), F32)] + [((half // wide, width), BF16)] * (wide - 1)
    got = shift(send, CORE, 2, 1)
    (keep,) = call(keep_kernel, [((half, width), F32)], [rest, held_weight])
    own, *sends = call(add_kernel, split, [place, keep, got], scalars=1)
    received = across(sends, 1)
    chunk = [((deep, row_dev, width), BF16)]
    (summed,) = call(sum_kernel, chunk, [own, *received])
    mixed = lax.all_to_all(summed, DEEP, 0, 0, tiled=True)
    hidden, payload = call(
        hidden_kernel,
        [((row_dev, width), BF16), ((deep, row_dev, full), BF16)],
        [mixed, residual, expert_ids, route_weights],
    )
    near = lax.all_to_all(payload, DEEP, 0, 0, tiled=True).reshape(deep * row_dev, full)
    share_slots = slots // wide
    pick, *parts = call(
        select_kernel,
        [((deep * row_dev, slots), BF16)] + [((share_slots, full), BF16)] * wide,
        [place, near],
        scalars=1,
    )
    parts = [parts[0]] + across(parts[1:], 1)
    low, send = call(sort_kernel, [((slots // 2, full), BF16)] * 2, parts)
    lows, highs = around(low, shift(send, CORE, 2, 1), mirrored)
    weights = [norm_gain.reshape(ring, 1, width), gate_matrix[0], up_matrix[0]]
    sums = [((slots, hidden_units), F32)] * 2
    partial = call(own_kernel, sums, [place, lows[0], highs[0], *weights], scalars=1)
    *partial, squares, share = call(
        near_kernel,
        sums + [((slots, TAIL), F32)] * 2,
        [place, *partial]
        + [lows[0], highs[0], lows[1], highs[1], lows[3], highs[3]]
        + weights,
        scalars=1,
    )
    (active,) = call(
        expert_kernel,
        [((slots, hidden_units), BF16)],
        [place, *partial, squares, lows[2], highs[2], *weights],
        scalars=1,
    )
    active2 = shift(active, CONTEXT, ring, 2)
    active1, active3 = (shift(active, CONTEXT, ring, step) for step in (1, 3))
    (made,) = call(
        first_kernel,
        [((slots, width), F32)],
        [place, active, active1, active3, others[0], others[2], down_matrix[0]],
        scalars=1,
    )
    low, high = call(
        down_kernel,
        [((slots // 2, width), BF16)] * 2,
        [made, active2, others[1], share],
    )
    parts = call(
        back_kernel,
        [((share_slots, width), BF16)] * wide,
        [low, shift(high, CORE, 2, 1)],
    )
    parts = [parts[0]] + across(parts[1:], -1)
    (summed,) = call(spread_kernel, chunk, [pick, *parts])
    returned = lax.all_to_all(summed, DEEP, 0, 0, tiled=True)
    done = [((row_dev, width), BF16)]
    return call(output_kernel, done, [returned, hidden], out=jax.ShapeDtypeStruct)[0]


def solution(mesh):
    fine = Mesh(mesh.devices.reshape(4, 4, 8, 2), (CONTEXT, WIDE, DEEP, CORE))
    return jax.shard_map(
        local,
        mesh=fine,
        in_specs=(
            P(None, EXPERT),
            P(EXPERT, None, None),
            P(EXPERT, None, None),
            P(CONTEXT, None, None),
            P(CONTEXT, None, None),
            P(),
            P(),
            P(),
            P(EXPERT, CONTEXT),
            P(EXPERT, CONTEXT),
            P(),
            P(EXPERT, None),
            P(EXPERT, None),
            P(EXPERT, None, CONTEXT),
            P(EXPERT, None, CONTEXT),
            P(EXPERT, CONTEXT, None),
        ),
        out_specs=P(EXPERT, CONTEXT),
        check_vma=False,
    )
```
